128 devices in a mesh: skyx: 4 (over z_lo, core), skyy: 8 (over z_hi, y), be: 4 (over x).
Axes of the slice: x: 4, y: 4, z: 4 (z_hi: 2, z_lo: 2; z = z_hi * 2 + z_lo), core: 2. Of those that a mesh axis runs over, the one named last changes fastest.
Arguments:
- image: float32 [4, 1024, 2048], P('be', 'skyx', 'skyy'), may hold values from -6 to 6
- psf_taps: float32 [4, 2, 15], P('be'), may hold values from 0.1 to 1
- exposure_weight: float32 [4], P('be'), may hold values from 0.5 to 4
- flux_start: float32 [4, 8, 16], P('skyx', 'skyy'), may hold values from 1 to 4
- centre_shift: float32 [2, 4, 8, 16], P(None, 'skyx', 'skyy'), may hold values from -0.5 to 0.5
- radius: float32 [4, 8, 16], P('skyx', 'skyy'), may hold values from 1.5 to 6
- ellipticity: float32 [2, 4, 8, 16], P(None, 'skyx', 'skyy'), may hold values from -0.4 to 0.4
- offsets: int32 [2, 4, 8, 16], P(None, 'skyx', 'skyy'), may hold values from -32 to 223, as said below
- source_count: int32 [4, 8], P('skyx', 'skyy'), may hold values from 4 to 16, as said below
Outputs:
- refined: float32 [3, 4, 8, 16], P(None, 'skyx', 'skyy')
- residual: float32 [4, 1024, 2048], P('be', 'skyx', 'skyy')
The draws below stay inside these ranges and needn't reach their ends.
Inputs may be any that keep to these rules, and one draw needn't show every extreme that they name: `offsets`: stamp corners in the tile's own pixels; a stamp's middle pixel lies in its tile; among the live sources of a tile at most 4 have stamps that reach past the tile's edge, and some tile has exactly 4. Slots 0 to source_count - 1 of a tile hold its sources and the rest are empty; some tile is full.
All inputs are finite; a program needn't handle non-finite values.
Results may differ from the reference program's by a relative error of at most 0.0003.
Values sent between devices are 32-bit elements; how exact they have to be, the bound alone decides.
A program may use at most 64 MiB of HBM per device.

```python
import math
import jax
import jax.numpy as jnp
from jax import lax

TILE = 256
S_DEV = 16
STAMP = 64
TAPS = 15
EXP = 4
HALF = 32
BMAX = 4
TILES_X = 4
TILES_Y = 8
PIX_X = 1024
PIX_Y = 2048


def layout_draw(key):
    keys = [jax.random.fold_in(key, 300 + index) for index in range(8)]
    tiles = (TILES_X, TILES_Y)
    counts = jax.random.randint(keys[0], tiles, S_DEV // 4, S_DEV + 1).astype(jnp.int32)
    counts = counts.at[0, 0].set(S_DEV)
    slot_index = jnp.arange(S_DEV, dtype=jnp.int32)
    live = slot_index[None, None, :] < counts[:, :, None]
    scores = jax.random.randint(keys[2], tiles + (S_DEV,), 0, 4096).astype(jnp.int32) * S_DEV + slot_index
    scores = jnp.where(live, scores, 4096 * S_DEV + slot_index)
    order = jnp.argsort(scores, axis=-1)
    ranks = jnp.argsort(order, axis=-1).astype(jnp.int32)
    border = ranks < BMAX
    interior = jax.random.randint(keys[3], (2,) + tiles + (S_DEV,), 0, TILE - STAMP + 1).astype(jnp.int32)
    sides = ranks % 4
    depth = ranks // 4 % 4
    low_side = depth - HALF
    high_side = TILE - HALF - 1 - depth
    across = jnp.where(sides % 2 == 0, low_side, high_side)
    other = jax.random.randint(keys[7], tiles + (S_DEV,), -HALF, TILE - HALF).astype(jnp.int32)
    first_dim = sides // 2 == 0
    corner_x = jnp.where(border, jnp.where(first_dim, across, other), interior[0])
    corner_y = jnp.where(border, jnp.where(first_dim, other, across), interior[1])
    return (counts, jnp.stack([corner_x, corner_y]).astype(jnp.int32))


def draw_offsets(key, part):
    return layout_draw(key)[1]


def draw_source_count(key, part):
    return layout_draw(key)[0]


def levels(own_key, dims, pieces, smallest, largest):
    factor_of = 1.0
    for position, parts in pieces:
        steps = jax.random.uniform(jax.random.fold_in(jax.random.fold_in(own_key, 6), position), (parts,), jnp.float32, smallest / len(pieces), largest / len(pieces))
        factor_of = factor_of * jnp.repeat(jnp.exp(steps), dims[position] // parts).reshape((-1,) + (1,) * (len(dims) - 1 - position))
    return factor_of


def scatter_about(rng, shape, spread, bound, shards=(), kind=jnp.bfloat16):
    result = spread * jax.random.normal(rng, shape, jnp.float32)
    if shards:
        result = result * levels(rng, shape, shards, -0.22, 0.18)
    return jnp.clip(result, -bound, bound).astype(kind)


def setup_inputs(seed: int = 0) -> dict:
    key_of = jax.random.split(jax.random.key(seed), 10)
    image = scatter_about(key_of[0], (EXP, PIX_X, PIX_Y), 1.0, 6.0, ((0, 4), (1, 4), (2, 8)), jnp.float32)
    psf_taps = jnp.clip(0.1 + 0.9 * jax.random.uniform(key_of[1], (EXP, 2, TAPS), jnp.float32) ** levels(key_of[1], (EXP, 2, TAPS), ((0, 4),), -0.2, 0.2), 0.1, 1.0)
    exposure_weight = jnp.clip(jnp.exp(math.log(4.0) - 2.0794415 * jax.random.uniform(key_of[2], (EXP,), jnp.float32) ** levels(key_of[2], (EXP,), ((0, 4),), -0.2, 0.2)), 0.5, 4.0)
    flux_start = jnp.clip(jnp.exp(math.log(4.0) - 1.3862944 * jax.random.uniform(key_of[3], (TILES_X, TILES_Y, S_DEV), jnp.float32) ** levels(key_of[3], (TILES_X, TILES_Y, S_DEV), ((0, 4), (1, 8)), -0.2, 0.2)), 1.0, 4.0)
    centre_shift = jnp.clip(jax.random.uniform(key_of[4], (2, TILES_X, TILES_Y, S_DEV), jnp.float32, -0.5, 0.5) * levels(key_of[4], (2, TILES_X, TILES_Y, S_DEV), ((1, 4), (2, 8)), -0.4, 0.0), -0.5, 0.5)
    radius = jnp.clip(jnp.exp(math.log(6.0) - 1.3862944 * jax.random.uniform(key_of[5], (TILES_X, TILES_Y, S_DEV), jnp.float32) ** levels(key_of[5], (TILES_X, TILES_Y, S_DEV), ((0, 4), (1, 8)), -0.2, 0.2)), 1.5, 6.0)
    ellipticity = jnp.clip(jax.random.uniform(key_of[6], (2, TILES_X, TILES_Y, S_DEV), jnp.float32, -0.4, 0.4) * levels(key_of[6], (2, TILES_X, TILES_Y, S_DEV), ((1, 4), (2, 8)), -0.4, 0.0), -0.4, 0.4)
    offsets = draw_offsets(jax.random.fold_in(key_of[9], 71), 0)
    source_count = draw_source_count(jax.random.fold_in(key_of[9], 71), 0)
    return dict(image=image, psf_taps=psf_taps, exposure_weight=exposure_weight, flux_start=flux_start, centre_shift=centre_shift, radius=radius, ellipticity=ellipticity, offsets=offsets, source_count=source_count)


HIGHEST = lax.Precision.HIGHEST
PRIOR = 8.0

def psf_matrix(taps, size):
    width = taps.shape[0]
    reach = (width - 1) // 2
    grid = jnp.arange(size, dtype=jnp.int32)
    differ = grid[:, None] - grid[None, :] + reach
    picks = (differ[:, :, None] == jnp.arange(width, dtype=jnp.int32)[None, None, :]).astype(jnp.float32)
    return lax.optimization_barrier(jnp.sum(picks * taps[None, None, :], axis=-1)) / jnp.sum(taps)

def profiles(shift_x, shift_y, radius, ellipse_one, ellipse_two, size):
    grid = jnp.arange(size, dtype=jnp.float32)
    middle = float(size // 2)
    along_x = grid[:, None] - (middle + shift_x)[None, :]
    along_y = grid[None, :] - (middle + shift_y)[:, None]
    inverse = 1.0 / (radius * radius)
    coef_a = ((1.0 + ellipse_one) * inverse)[None, :, None]
    coef_b = (ellipse_two * inverse)[None, :, None]
    coef_c = ((1.0 - ellipse_one) * inverse)[None, :, None]
    upper = along_x[:, :, None]
    lower = along_y[None, :, :]
    root = jnp.sqrt(coef_a * upper * upper + 2.0 * coef_b * upper * lower + coef_c * lower * lower + 0.25)
    profile = jnp.exp(-root)
    return (profile, profile * (coef_a * upper + coef_b * lower) / root, profile * (coef_b * upper + coef_c * lower) / root)

def blur(stack, first, second):
    size = stack.shape[0]
    along_rows = jnp.dot(first, stack.reshape(size, -1), precision=HIGHEST, preferred_element_type=jnp.float32)
    along_columns = jnp.dot(along_rows.reshape(-1, size), second.T, precision=HIGHEST, preferred_element_type=jnp.float32)
    return along_columns.reshape(stack.shape)

def place(canvas, stamps, row_index, column_index):
    height = canvas.shape[0]
    width = canvas.shape[1]
    row_index = jnp.where((row_index >= 0) & (row_index < height), row_index, height)
    column_index = jnp.where((column_index >= 0) & (column_index < width), column_index, width)
    return canvas.at[row_index[:, :, None], column_index[None, :, :]].add(stamps, mode='drop')

def solve_three(matrix, right):

    def adjugate(row, column):
        return matrix[(column + 1) % 3, (row + 1) % 3] * matrix[(column + 2) % 3, (row + 2) % 3] - matrix[(column + 1) % 3, (row + 2) % 3] * matrix[(column + 2) % 3, (row + 1) % 3]
    determinant = matrix[0, 0] * adjugate(0, 0) + matrix[0, 1] * adjugate(1, 0) + matrix[0, 2] * adjugate(2, 0)
    return jnp.stack([(adjugate(row, 0) * right[0] + adjugate(row, 1) * right[1] + adjugate(row, 2) * right[2]) / determinant for row in range(3)])

def reference(image, psf_taps, exposure_weight, flux_start, centre_shift, radius, ellipticity, offsets, source_count):
    tiles_x = flux_start.shape[0]
    tiles_y = flux_start.shape[1]
    slots = flux_start.shape[2]
    tile = image.shape[1] // tiles_x
    stamp = STAMP
    live = (jnp.arange(slots, dtype=jnp.int32)[None, None, :] < source_count[:, :, None]).astype(jnp.float32).reshape(-1)
    flux = flux_start.reshape(-1) * live
    shift_x = centre_shift[0].reshape(-1)
    shift_y = centre_shift[1].reshape(-1)
    local_x = offsets[0].reshape(-1)
    local_y = offsets[1].reshape(-1)
    base_x = (jnp.arange(tiles_x, dtype=jnp.int32)[:, None, None] * tile + offsets[0]).reshape(-1)
    base_y = (jnp.arange(tiles_y, dtype=jnp.int32)[None, :, None] * tile + offsets[1]).reshape(-1)
    grid = jnp.arange(stamp, dtype=jnp.int32)
    row_index = grid[:, None] + base_x[None, :]
    column_index = base_y[:, None] + grid[None, :]
    inside_x = ((grid[:, None] + local_x[None, :] >= 0) & (grid[:, None] + local_x[None, :] < tile)).astype(jnp.float32)
    inside_y = ((local_y[:, None] + grid[None, :] >= 0) & (local_y[:, None] + grid[None, :] < tile)).astype(jnp.float32)
    mask = inside_x[:, :, None] * inside_y[None, :, :]
    profile, slope_x, slope_y = profiles(shift_x, shift_y, radius.reshape(-1), ellipticity[0].reshape(-1), ellipticity[1].reshape(-1), stamp)
    rows_clipped = jnp.clip(row_index, 0, image.shape[1] - 1)
    columns_clipped = jnp.clip(column_index, 0, image.shape[2] - 1)
    count = flux.shape[0]
    normal = jnp.zeros((3, 3, count), jnp.float32)
    right = jnp.zeros((3, count), jnp.float32)
    residuals = []
    weighted_flux = flux[None, :, None]
    for exposure in range(image.shape[0]):
        first = psf_matrix(psf_taps[exposure, 0], stamp)
        second = psf_matrix(psf_taps[exposure, 1], stamp)
        blurred = blur(profile, first, second)
        canvas = place(jnp.zeros(image.shape[1:], jnp.float32), blurred * weighted_flux, row_index, column_index)
        remain = image[exposure] - canvas
        residuals.append(remain)
        jacobian = jnp.stack([blurred * mask, blur(slope_x, first, second) * weighted_flux * mask, blur(slope_y, first, second) * weighted_flux * mask])
        cutout = remain[rows_clipped[:, :, None], columns_clipped[None, :, :]]
        normal = normal + exposure_weight[exposure] * jnp.einsum('kisj,lisj->kls', jacobian, jacobian, precision=HIGHEST)
        right = right + exposure_weight[exposure] * jnp.einsum('kisj,isj->ks', jacobian, cutout, precision=HIGHEST)
    identity = jnp.eye(3, dtype=jnp.float32)[:, :, None]
    change = solve_three(normal + PRIOR * identity, right)
    refined = jnp.stack([flux_start.reshape(-1) + change[0], shift_x + change[1], shift_y + change[2]]) * live[None, :]
    return (refined.reshape(3, tiles_x, tiles_y, slots), jnp.stack(residuals))
```

```python
import jax
import jax.numpy as jnp
from jax import lax
from jax.experimental import pallas as pl
from jax.experimental.pallas import tpu as pltpu
from jax.sharding import PartitionSpec as P

STAMP = 64
MARGIN = 32
TAPS = 15
PRIOR = 8.0
F32 = jnp.float32
BF16 = jnp.bfloat16
MESH = pl.DeviceIdType.MESH


def split(x):
    high = x.astype(BF16)
    return high, (x - high.astype(F32)).astype(BF16)


def band(taps_ref, which, differ):
    total = taps_ref[0, which, 0]
    for t in range(1, TAPS):
        total = total + taps_ref[0, which, t]
    out = jnp.zeros(differ.shape, F32)
    for t in range(TAPS):
        out = jnp.where(differ == t - TAPS // 2, taps_ref[0, which, t], out)
    return out / jnp.full(differ.shape, total, F32)


def kernel(
    image_hbm,
    taps_ref,
    weight_ref,
    flux_ref,
    shift_ref,
    radius_ref,
    ellipse_ref,
    offset_ref,
    count_ref,
    flux_vec,
    shift_vec,
    refined_ref,
    residual_hbm,
    image,
    stacked,
    field,
    blurred,
    lanes_high,
    lanes_low,
    canvas,
    pack_left,
    pack_right,
    in_rows,
    in_sides,
    in_corners,
    remain,
    partial,
    sums,
    copy_sems,
    send_sems,
    recv_sems,
    sum_send,
    sum_recv,
):
    slots = flux_ref.shape[2]
    tile = image_hbm.shape[1]
    pairs = slots // 2
    mx = lax.axis_index("skyx")
    my = lax.axis_index("skyy")
    me = lax.axis_index("be")
    nx = lax.axis_size("skyx")
    ny = lax.axis_size("skyy")
    nb = lax.axis_size("be")
    up, down = lax.rem(mx + nx - 1, nx), lax.rem(mx + 1, nx)
    left, right = lax.rem(my + ny - 1, ny), lax.rem(my + 1, ny)
    around = [
        (up, my, me),
        (down, my, me),
        (mx, left, me),
        (mx, right, me),
        (up, left, me),
        (up, right, me),
        (down, left, me),
        (down, right, me),
    ]
    peers = [(mx, my, lax.rem(me + d, nb)) for d in range(1, nb)]

    barrier = pltpu.get_barrier_semaphore()
    for device in around + peers:
        pl.semaphore_signal(barrier, inc=1, device_id=device, device_id_type=MESH)
    fetch = pltpu.make_async_copy(image_hbm.at[0], image, copy_sems.at[0])
    fetch.start()

    row = lax.broadcasted_iota(jnp.int32, (STAMP, 128), 0)
    lane = lax.broadcasted_iota(jnp.int32, (STAMP, 128), 1)
    lane1 = lax.broadcasted_iota(jnp.int32, (1, 128), 1)
    first_half = lane1 < STAMP
    column1 = jnp.where(first_half, lane1, lane1 - STAMP)
    live_count = count_ref[0, 0]

    def pair_of(ref, *index):
        def at(j):
            return jnp.where(first_half, ref[index + (2 * j,)], ref[index + (2 * j + 1,)])

        return at

    rows_band = band(taps_ref, 0, row[:, :STAMP] - lane[:, :STAMP])
    rows_high, rows_low = split(rows_band)
    left_factor = jnp.concatenate([rows_high, rows_high, rows_low], axis=1)
    columns_band = jnp.where(lane < STAMP, band(taps_ref, 1, lane - row), 0.0)
    columns_next = pltpu.roll(columns_band, STAMP, 1)
    nothing = jnp.zeros((STAMP, 128), F32)
    right_factor = jnp.concatenate(
        [
            jnp.concatenate([columns_band, nothing], axis=1),
            jnp.concatenate([columns_next, nothing], axis=1),
            jnp.concatenate([nothing, columns_band], axis=1),
            jnp.concatenate([nothing, columns_next], axis=1),
        ],
        axis=0,
    )
    right_high, right_low = split(right_factor)

    def blur(count):
        width = count * slots * STAMP
        along = jnp.dot(left_factor, stacked[:, :width], preferred_element_type=F32)
        groups = jnp.concatenate(
            [along[:, 256 * g : 256 * (g + 1)] for g in range(width // 256)], axis=0
        )
        high, low = split(groups)
        out = jnp.dot(high, right_high, preferred_element_type=F32)
        out = out + jnp.dot(low, right_high, preferred_element_type=F32)
        return out + jnp.dot(high, right_low, preferred_element_type=F32)

    def stack(value, start):
        high, low = split(value)
        stacked[0:STAMP, start : start + 128] = high
        stacked[STAMP : 2 * STAMP, start : start + 128] = low
        stacked[2 * STAMP : 3 * STAMP, start : start + 128] = high

    grid_u = row.astype(F32)
    for j in range(pairs):
        shift_x = pair_of(shift_ref, 0, 0, 0)(j)
        shift_y = pair_of(shift_ref, 1, 0, 0)(j)
        radius = pair_of(radius_ref, 0, 0)(j)
        one = pair_of(ellipse_ref, 0, 0, 0)(j)
        two = pair_of(ellipse_ref, 1, 0, 0)(j)
        inverse = 1.0 / (radius * radius)
        coef_a = (1.0 + one) * inverse
        coef_b = two * inverse
        coef_c = (1.0 - one) * inverse
        u = grid_u - (float(STAMP // 2) + shift_x)
        v = column1.astype(F32) - (float(STAMP // 2) + shift_y)
        along_x = coef_a * u + coef_b * v
        along_y = coef_b * u + coef_c * v
        square = u * along_x + v * along_y + 0.25
        inverse_root = lax.rsqrt(square)
        profile = jnp.exp(-(square * inverse_root))
        stack(profile, 128 * j)
        scaled = profile * inverse_root
        field[0, :, 128 * j : 128 * (j + 1)] = scaled * along_x
        field[1, :, 128 * j : 128 * (j + 1)] = scaled * along_y

    spread = blur(1)
    for g in range(slots * STAMP // 256):
        blurred[0, :, 256 * g : 256 * (g + 1)] = spread[STAMP * g : STAMP * (g + 1)]

    targets = []
    for s in range(slots):
        flux = jnp.where(s < live_count, flux_ref[0, 0, s], 0.0)
        at_y = offset_ref[1, 0, 0, s]
        turn = jnp.bitwise_and(at_y, 127)
        block = jnp.right_shift(at_y - turn, 7)
        j, odd = s // 2, s % 2
        value = blurred[0, :, 128 * j : 128 * (j + 1)]
        value = jnp.where(first_half if odd == 0 else ~first_half, value * flux, 0.0)
        value = pltpu.roll(value, jnp.bitwise_and(turn + 128 - STAMP * odd, 127), 1)
        owner = jnp.where(lane1 >= turn, block, block + 1)
        owner = jnp.where(owner == -1, 2, owner)
        for g in range(3):
            high, low = split(jnp.where(owner == g, value, 0.0))
            lanes_high[STAMP * s : STAMP * (s + 1), 128 * g : 128 * (g + 1)] = high
            lanes_low[STAMP * s : STAMP * (s + 1), 128 * g : 128 * (g + 1)] = low
    for j in range(pairs):
        targets.append(pair_of(offset_ref, 0, 0, 0)(j) + column1 + MARGIN)
    target = jnp.concatenate(targets, axis=1)
    rows = tile + 2 * MARGIN
    place = jnp.where(
        lax.broadcasted_iota(jnp.int32, (rows, slots * STAMP), 0) == target, 1.0, 0.0
    ).astype(BF16)
    placed = jnp.dot(place, lanes_high[...], preferred_element_type=F32)
    placed = placed + jnp.dot(place, lanes_low[...], preferred_element_type=F32)
    canvas[...] = placed
    side = placed[MARGIN : MARGIN + tile, 256:384]
    to_left, to_right = None, None
    for c in range(4):
        chunk = side[64 * c : 64 * (c + 1)]
        here = (lane >= 32 * c) & (lane < 32 * (c + 1))
        moved = pltpu.roll(chunk, (32 * c + 128 - 96) % 128, 1)
        to_left = moved if c == 0 else jnp.where(here, moved, to_left)
        moved = pltpu.roll(chunk, 32 * c, 1) if c else chunk
        to_right = moved if c == 0 else jnp.where(here, moved, to_right)
    pack_left[...] = to_left
    pack_right[...] = to_right

    top = canvas.at[0:MARGIN]
    bottom = canvas.at[tile + MARGIN : tile + 2 * MARGIN]
    sources = [
        top.at[:, 0:tile],
        bottom.at[:, 0:tile],
        pack_left,
        pack_right,
        top.at[:, tile : tile + 128],
        top.at[:, tile : tile + 128],
        bottom.at[:, tile : tile + 128],
        bottom.at[:, tile : tile + 128],
    ]
    landings = [
        in_rows.at[0],
        in_rows.at[1],
        in_sides.at[0],
        in_sides.at[1],
        in_corners.at[0],
        in_corners.at[1],
        in_corners.at[2],
        in_corners.at[3],
    ]
    pl.semaphore_wait(barrier, len(around) + len(peers))
    halos = [
        pltpu.make_async_remote_copy(
            src_ref=sources[d],
            dst_ref=landings[d],
            send_sem=send_sems.at[d],
            recv_sem=recv_sems.at[d],
            device_id=around[d],
            device_id_type=MESH,
        )
        for d in range(8)
    ]
    for halo in halos:
        halo.start()

    for k in range(2):
        for j in range(pairs):
            stack(field[k, :, 128 * j : 128 * (j + 1)], 1024 * k + 128 * j)
    spread = blur(2)
    for k in range(2):
        for g in range(4):
            start = STAMP * (4 * k + g)
            blurred[1 + k, :, 256 * g : 256 * (g + 1)] = spread[start : start + STAMP]

    def fold(value):
        total = value[0:8]
        for r in range(8, STAMP, 8):
            total = total + value[r : r + 8]
        return total

    for j in range(pairs):
        at_x = row + pair_of(offset_ref, 0, 0, 0)(j)
        at_y = column1 + pair_of(offset_ref, 1, 0, 0)(j)
        inside = (at_x >= 0) & (at_x < tile) & (at_y >= 0) & (at_y < tile)
        own = slice(128 * j, 128 * (j + 1))
        masked = [jnp.where(inside, blurred[k, :, own], 0.0) for k in range(3)]
        for k in range(3):
            blurred[k, :, own] = masked[k]
        n = 0
        for k in range(3):
            for l in range(k, 3):
                partial[8 * n : 8 * (n + 1), own] = fold(masked[k] * masked[l])
                n += 1

    segment = jnp.where(
        jnp.right_shift(lax.broadcasted_iota(jnp.int32, (slots * STAMP, 128), 0), 6)
        == lax.broadcasted_iota(jnp.int32, (slots * STAMP, 128), 1),
        1.0,
        0.0,
    ).astype(BF16)

    def gather_sums(value):
        high, low = split(value)
        out = jnp.dot(high, segment, preferred_element_type=F32)
        out = out + jnp.dot(low, segment, preferred_element_type=F32)
        return jnp.concatenate(
            [
                jnp.sum(out[8 * k : 8 * (k + 1)], axis=0, keepdims=True)
                for k in range(value.shape[0] // 8)
            ],
            axis=0,
        )

    normal = gather_sums(partial[0:48, :])

    apart = lax.broadcasted_iota(jnp.int32, (STAMP, tile), 1) - lax.broadcasted_iota(
        jnp.int32, (STAMP, tile), 0
    )
    pick = jnp.concatenate(
        [
            jnp.where(apart == offset_ref[0, 0, 0, s], 1.0, 0.0).astype(BF16)
            for s in range(slots)
        ],
        axis=0,
    )

    fetch.wait()
    for halo in halos:
        halo.wait_recv()

    ones = jnp.ones((1, 128), jnp.int32)
    has_up = ones * (mx > 0).astype(jnp.int32) > 0
    has_down = ones * (mx < nx - 1).astype(jnp.int32) > 0
    has_left = ones * (my > 0).astype(jnp.int32) > 0
    has_right = ones * (my < ny - 1).astype(jnp.int32) > 0
    low_lanes = lane1 < MARGIN
    high_lanes = lane1 >= 128 - MARGIN
    for c in range(4):
        for g in range(2):
            r0 = 64 * c
            own = slice(128 * g, 128 * (g + 1))
            total = canvas[MARGIN + r0 : MARGIN + r0 + 64, own]
            if g == 0:
                moved = in_sides[1]
                moved = pltpu.roll(moved, 128 - 32 * c, 1) if c else moved
                total = total + jnp.where(low_lanes & has_left, moved, 0.0)
            else:
                moved = in_sides[0]
                moved = pltpu.roll(moved, 96 - 32 * c, 1) if c < 3 else moved
                total = total + jnp.where(high_lanes & has_right, moved, 0.0)
            if c == 0:
                edge = jnp.where(has_up, in_rows[1, :, own], 0.0)
                if g == 0:
                    edge = edge + jnp.where(low_lanes & has_up & has_left, in_corners[3], 0.0)
                else:
                    edge = edge + jnp.where(high_lanes & has_up & has_right, in_corners[2], 0.0)
                total = jnp.concatenate([total[0:32] + edge, total[32:64]], axis=0)
            if c == 3:
                edge = jnp.where(has_down, in_rows[0, :, own], 0.0)
                if g == 0:
                    edge = edge + jnp.where(low_lanes & has_down & has_left, in_corners[1], 0.0)
                else:
                    edge = edge + jnp.where(high_lanes & has_down & has_right, in_corners[0], 0.0)
                total = jnp.concatenate([total[0:32], total[32:64] + edge], axis=0)
            remain[r0 : r0 + 64, own] = image[r0 : r0 + 64, own] - total
    store = pltpu.make_async_copy(remain, residual_hbm.at[0], copy_sems.at[1])
    store.start()

    high, low = split(remain[...])
    strips = jnp.dot(pick, high, preferred_element_type=F32)
    strips = strips + jnp.dot(pick, low, preferred_element_type=F32)
    for j in range(pairs):
        halves = []
        for odd in range(2):
            s = 2 * j + odd
            at_y = offset_ref[1, 0, 0, s]
            turn = jnp.bitwise_and(at_y, 127)
            block = jnp.right_shift(at_y - turn, 7)
            strip = strips[STAMP * s : STAMP * (s + 1)]
            take_one = jnp.where(lane1 >= turn, block, block + 1) >= 1
            value = jnp.where(take_one, strip[:, 128:256], strip[:, 0:128])
            halves.append(
                pltpu.roll(value, jnp.bitwise_and(STAMP * odd + 256 - turn, 127), 1)
            )
        cutout = jnp.where(first_half, halves[0], halves[1])
        own = slice(128 * j, 128 * (j + 1))
        for k in range(3):
            partial[48 + 8 * k : 56 + 8 * k, own] = fold(blurred[k, :, own] * cutout)
    rights = gather_sums(partial[48:72, :])
    weight = weight_ref[0]
    sums[me] = weight * jnp.concatenate([normal, rights, jnp.zeros((7, 128), F32)], axis=0)

    shares = []
    for d in range(1, nb):
        share = pltpu.make_async_remote_copy(
            src_ref=sums.at[me],
            dst_ref=sums.at[me],
            send_sem=sum_send.at[d - 1],
            recv_sem=sum_recv.at[d - 1],
            device_id=peers[d - 1],
            device_id_type=MESH,
        )
        share.start()
        shares.append(share)
    for d in range(1, nb):
        source = lax.rem(me + nb - d, nb)
        pltpu.make_async_remote_copy(
            src_ref=sums.at[source],
            dst_ref=sums.at[source],
            send_sem=sum_send.at[d - 1],
            recv_sem=sum_recv.at[d - 1],
            device_id=peers[d - 1],
            device_id_type=MESH,
        ).wait_recv()
    total = sums[0]
    for e in range(1, nb):
        total = total + sums[e]

    live = lax.broadcasted_iota(jnp.int32, (1, slots), 1) < live_count
    start = flux_vec[0]
    flux = jnp.where(live, start, 0.0)
    entry = [total[n : n + 1, 0:slots] for n in range(9)]
    m01, m02 = entry[1] * flux, entry[2] * flux
    m12 = entry[4] * flux * flux
    m00 = entry[0] + PRIOR
    m11 = entry[3] * flux * flux + PRIOR
    m22 = entry[5] * flux * flux + PRIOR
    v0, v1, v2 = entry[6], entry[7] * flux, entry[8] * flux
    c00 = m11 * m22 - m12 * m12
    c01 = m12 * m02 - m01 * m22
    c02 = m01 * m12 - m11 * m02
    c11 = m00 * m22 - m02 * m02
    c12 = m01 * m02 - m00 * m12
    c22 = m00 * m11 - m01 * m01
    determinant = m00 * c00 + m01 * c01 + m02 * c02
    change = [
        (c00 * v0 + c01 * v1 + c02 * v2) / determinant,
        (c01 * v0 + c11 * v1 + c12 * v2) / determinant,
        (c02 * v0 + c12 * v1 + c22 * v2) / determinant,
    ]
    bases = [start, shift_vec[0, 0], shift_vec[1, 0]]
    for k in range(3):
        refined_ref[k, 0] = jnp.where(live, bases[k] + change[k], 0.0)

    for share in shares:
        share.wait_send()
    for halo in halos:
        halo.wait_send()
    store.wait()


def shards(
    image,
    psf_taps,
    exposure_weight,
    flux_start,
    centre_shift,
    radius,
    ellipticity,
    offsets,
    source_count,
):
    tile = image.shape[1]
    slots = flux_start.shape[2]
    rows = tile + 2 * MARGIN
    width = slots * STAMP
    smem = pl.BlockSpec(memory_space=pltpu.SMEM)
    vmem = pl.BlockSpec(memory_space=pltpu.VMEM)
    hbm = pl.BlockSpec(memory_space=pl.ANY)
    peers = lax.axis_size("be") - 1
    return pl.pallas_call(
        kernel,
        out_shape=(
            jax.ShapeDtypeStruct((3, 1, 1, slots), F32),
            jax.ShapeDtypeStruct(image.shape, F32),
        ),
        in_specs=[hbm] + [smem] * 8 + [vmem] * 2,
        out_specs=(vmem, hbm),
        scratch_shapes=[
            pltpu.VMEM((tile, tile), F32),
            pltpu.VMEM((3 * STAMP, 2 * width), BF16),
            pltpu.VMEM((2, STAMP, width), F32),
            pltpu.VMEM((3, STAMP, width), F32),
            pltpu.VMEM((width, 384), BF16),
            pltpu.VMEM((width, 384), BF16),
            pltpu.VMEM((rows, 384), F32),
            pltpu.VMEM((STAMP, 128), F32),
            pltpu.VMEM((STAMP, 128), F32),
            pltpu.VMEM((2, MARGIN, tile), F32),
            pltpu.VMEM((2, STAMP, 128), F32),
            pltpu.VMEM((4, MARGIN, 128), F32),
            pltpu.VMEM((tile, tile), F32),
            pltpu.VMEM((72, width), F32),
            pltpu.VMEM((peers + 1, 16, 128), F32),
            pltpu.SemaphoreType.DMA((2,)),
            pltpu.SemaphoreType.DMA((8,)),
            pltpu.SemaphoreType.DMA((8,)),
            pltpu.SemaphoreType.DMA((peers,)),
            pltpu.SemaphoreType.DMA((peers,)),
        ],
        compiler_params=pltpu.CompilerParams(collective_id=0, has_side_effects=True),
        name="photometry",
    )(
        image,
        psf_taps,
        exposure_weight,
        flux_start,
        centre_shift,
        radius,
        ellipticity,
        offsets,
        source_count,
        flux_start,
        centre_shift,
    )


def solution(mesh):
    return jax.shard_map(
        shards,
        mesh=mesh,
        in_specs=(
            P("be", "skyx", "skyy"),
            P("be", None, None),
            P("be"),
            P("skyx", "skyy", None),
            P(None, "skyx", "skyy", None),
            P("skyx", "skyy", None),
            P(None, "skyx", "skyy", None),
            P(None, "skyx", "skyy", None),
            P("skyx", "skyy"),
        ),
        out_specs=(P(None, "skyx", "skyy", None), P("be", "skyx", "skyy")),
        check_vma=False,
    )
```

```python
import jax
import jax.numpy as jnp
from jax import lax
from jax.experimental import pallas as pl
from jax.experimental.pallas import tpu as pltpu
from jax.sharding import PartitionSpec as P

STAMP = 64
MARGIN = 32
TAPS = 15
PRIOR = 8.0
F32 = jnp.float32
BF16 = jnp.bfloat16
MESH = pl.DeviceIdType.MESH


def split(x):
    high = x.astype(BF16)
    return high, (x - high.astype(F32)).astype(BF16)


def band(taps_ref, which, differ):
    total = taps_ref[0, which, 0]
    for t in range(1, TAPS):
        total = total + taps_ref[0, which, t]
    out = jnp.zeros(differ.shape, F32)
    for t in range(TAPS):
        out = jnp.where(differ == t - TAPS // 2, taps_ref[0, which, t], out)
    return out / jnp.full(differ.shape, total, F32)


def kernel(
    image_hbm,
    taps_hbm,
    weight_hbm,
    flux_hbm,
    shift_hbm,
    radius_hbm,
    ellipse_hbm,
    offset_hbm,
    count_hbm,
    sums_ref,
    remain_ref,
    taps_ref,
    weight_ref,
    flux_ref,
    shift_ref,
    radius_ref,
    ellipse_ref,
    offset_ref,
    count_ref,
    flux_vec,
    shift_vec,
    image,
    stacked,
    field,
    blurred,
    lanes_high,
    lanes_low,
    canvas,
    pack_sides,
    pack_corners,
    in_rows,
    in_sides,
    in_corners,
    partial,
    sums,
    copy_sems,
    send_sems,
    recv_sems,
    sum_send,
    sum_recv,
):
    slots = flux_hbm.shape[2]
    tile = image_hbm.shape[1]
    pairs = slots // 2
    mx = lax.axis_index("skyx")
    my = lax.axis_index("skyy")
    me = lax.axis_index("be")
    nx = lax.axis_size("skyx")
    ny = lax.axis_size("skyy")
    nb = lax.axis_size("be")
    above, below = (mx > 0).astype(jnp.int32), (mx < nx - 1).astype(jnp.int32)
    before, after = (my > 0).astype(jnp.int32), (my < ny - 1).astype(jnp.int32)
    around = [
        (mx - above, my, me),
        (mx + below, my, me),
        (mx, my - before, me),
        (mx, my + after, me),
        (mx - above, my - before, me),
        (mx - above, my + after, me),
        (mx + below, my - before, me),
        (mx + below, my + after, me),
    ]
    exists = [
        above,
        below,
        before,
        after,
        above * before,
        above * after,
        below * before,
        below * after,
    ]
    peers = [(mx, my, lax.rem(me + d, nb)) for d in range(1, nb)]

    barrier = pltpu.get_barrier_semaphore()
    for device in peers:
        pl.semaphore_signal(barrier, inc=1, device_id=device, device_id_type=MESH)
    for device, there in zip(around, exists):

        @pl.when(there == 1)
        def _():
            pl.semaphore_signal(barrier, inc=1, device_id=device, device_id_type=MESH)

    small = [
        (offset_hbm, offset_ref),
        (shift_hbm, shift_ref),
        (radius_hbm, radius_ref),
        (ellipse_hbm, ellipse_ref),
        (taps_hbm, taps_ref),
        (flux_hbm, flux_ref),
        (count_hbm, count_ref),
        (weight_hbm, weight_ref),
        (flux_hbm, flux_vec),
        (shift_hbm, shift_vec),
    ]
    fetches = [
        pltpu.make_async_copy(source, target, copy_sems.at[n + 1])
        for n, (source, target) in enumerate(small)
    ]
    for fetch in fetches:
        fetch.start()
    fetch_image = pltpu.make_async_copy(image_hbm.at[0], image, copy_sems.at[0])
    fetch_image.start()
    for fetch in fetches:
        fetch.wait()

    row = lax.broadcasted_iota(jnp.int32, (STAMP, 128), 0)
    lane = lax.broadcasted_iota(jnp.int32, (STAMP, 128), 1)
    lane1 = lax.broadcasted_iota(jnp.int32, (1, 128), 1)
    first_half = lane1 < STAMP
    column1 = jnp.where(first_half, lane1, lane1 - STAMP)
    live_count = count_ref[0, 0]

    def pair_of(ref, *index):
        def at(j):
            return jnp.where(first_half, ref[index + (2 * j,)], ref[index + (2 * j + 1,)])

        return at

    rows_band = band(taps_ref, 0, row[:, :STAMP] - lane[:, :STAMP])
    rows_high, rows_low = split(rows_band)
    left_factor = jnp.concatenate([rows_high, rows_high, rows_low], axis=1)
    columns_band = jnp.where(lane < STAMP, band(taps_ref, 1, lane - row), 0.0)
    columns_next = pltpu.roll(columns_band, STAMP, 1)
    nothing = jnp.zeros((STAMP, 128), F32)
    right_factor = jnp.concatenate(
        [
            jnp.concatenate([columns_band, nothing], axis=1),
            jnp.concatenate([columns_next, nothing], axis=1),
            jnp.concatenate([nothing, columns_band], axis=1),
            jnp.concatenate([nothing, columns_next], axis=1),
        ],
        axis=0,
    )
    right_high, right_low = split(right_factor)

    def blur(count):
        width = count * slots * STAMP
        along = jnp.dot(left_factor, stacked[:, :width], preferred_element_type=F32)
        groups = jnp.concatenate(
            [along[:, 256 * g : 256 * (g + 1)] for g in range(width // 256)], axis=0
        )
        high, low = split(groups)
        out = jnp.dot(high, right_high, preferred_element_type=F32)
        out = out + jnp.dot(low, right_high, preferred_element_type=F32)
        return out + jnp.dot(high, right_low, preferred_element_type=F32)

    def stack(value, start):
        high, low = split(value)
        stacked[0:STAMP, start : start + 128] = high
        stacked[STAMP : 2 * STAMP, start : start + 128] = low
        stacked[2 * STAMP : 3 * STAMP, start : start + 128] = high

    grid_u = row.astype(F32)
    for j in range(pairs):
        shift_x = pair_of(shift_ref, 0, 0, 0)(j)
        shift_y = pair_of(shift_ref, 1, 0, 0)(j)
        radius = pair_of(radius_ref, 0, 0)(j)
        one = pair_of(ellipse_ref, 0, 0, 0)(j)
        two = pair_of(ellipse_ref, 1, 0, 0)(j)
        inverse = 1.0 / (radius * radius)
        coef_a = (1.0 + one) * inverse
        coef_b = two * inverse
        coef_c = (1.0 - one) * inverse
        u = grid_u - (float(STAMP // 2) + shift_x)
        v = column1.astype(F32) - (float(STAMP // 2) + shift_y)
        along_x = coef_a * u + coef_b * v
        along_y = coef_b * u + coef_c * v
        square = u * along_x + v * along_y + 0.25
        inverse_root = lax.rsqrt(square)
        profile = jnp.exp(-(square * inverse_root))
        stack(profile, 128 * j)
        scaled = profile * inverse_root
        field[0, :, 128 * j : 128 * (j + 1)] = scaled * along_x
        field[1, :, 128 * j : 128 * (j + 1)] = scaled * along_y

    spread = blur(1)
    for g in range(slots * STAMP // 256):
        blurred[0, :, 256 * g : 256 * (g + 1)] = spread[STAMP * g : STAMP * (g + 1)]

    targets = []
    for s in range(slots):
        flux = jnp.where(s < live_count, flux_ref[0, 0, s], 0.0)
        at_y = offset_ref[1, 0, 0, s]
        turn = jnp.bitwise_and(at_y, 127)
        block = jnp.right_shift(at_y - turn, 7)
        j, odd = s // 2, s % 2
        value = blurred[0, :, 128 * j : 128 * (j + 1)]
        value = jnp.where(first_half if odd == 0 else ~first_half, value * flux, 0.0)
        value = pltpu.roll(value, jnp.bitwise_and(turn + 128 - STAMP * odd, 127), 1)
        owner = jnp.where(lane1 >= turn, block, block + 1)
        owner = jnp.where(owner == -1, 2, owner)
        high, low = split(value)
        for g in range(3):
            keep = jnp.where(owner == g, 1.0, 0.0).astype(BF16)
            lanes_high[STAMP * s : STAMP * (s + 1), 128 * g : 128 * (g + 1)] = high * keep
            lanes_low[STAMP * s : STAMP * (s + 1), 128 * g : 128 * (g + 1)] = low * keep
    for j in range(pairs):
        targets.append(pair_of(offset_ref, 0, 0, 0)(j) + column1 + MARGIN)
    target = jnp.concatenate(targets, axis=1)
    rows = tile + 2 * MARGIN
    place = jnp.where(
        lax.broadcasted_iota(jnp.int32, (rows, slots * STAMP), 0) == target, 1.0, 0.0
    ).astype(BF16)
    placed = jnp.dot(place, lanes_high[...], preferred_element_type=F32)
    placed = placed + jnp.dot(place, lanes_low[...], preferred_element_type=F32)
    canvas[...] = placed

    def pack(strip, first_lane):
        size = strip.shape[0] // 4
        place_in = lax.broadcasted_iota(jnp.int32, (size, 128), 1)
        out = None
        for c in range(4):
            turn = (32 * c + 128 - first_lane) % 128
            block = strip[size * c : size * (c + 1)]
            block = pltpu.roll(block, turn, 1) if turn else block
            out = block if c == 0 else jnp.where(place_in >= 32 * c, block, out)
        return out

    side = placed[:, tile : tile + 128]
    bands = [side[MARGIN : MARGIN + tile], side[0:MARGIN], side[MARGIN + tile :]]
    pack_sides[0] = pack(bands[0], 96)
    pack_sides[1] = pack(bands[0], 0)
    pack_corners[0] = pack(bands[1], 96)
    pack_corners[1] = pack(bands[1], 0)
    pack_corners[2] = pack(bands[2], 96)
    pack_corners[3] = pack(bands[2], 0)

    sources = [canvas.at[0:MARGIN, 0:tile], canvas.at[tile + MARGIN :, 0:tile]]
    sources += [pack_sides.at[d] for d in range(2)] + [pack_corners.at[d] for d in range(4)]
    landings = [in_rows.at[d] for d in range(2)] + [in_sides.at[d] for d in range(2)]
    landings += [in_corners.at[d] for d in range(4)]
    pl.semaphore_wait(barrier, len(peers) + sum(exists))
    halos = [
        pltpu.make_async_remote_copy(
            src_ref=sources[d],
            dst_ref=landings[d],
            send_sem=send_sems.at[d],
            recv_sem=recv_sems.at[d],
            device_id=around[d],
            device_id_type=MESH,
        )
        for d in range(8)
    ]
    for halo, there in zip(halos, exists):

        @pl.when(there == 1)
        def _():
            halo.start()

    for k in range(2):
        for j in range(pairs):
            stack(field[k, :, 128 * j : 128 * (j + 1)], 1024 * k + 128 * j)
    spread = blur(2)
    for k in range(2):
        for g in range(4):
            start = STAMP * (4 * k + g)
            blurred[1 + k, :, 256 * g : 256 * (g + 1)] = spread[start : start + STAMP]

    def fold(value):
        total = value[0:8]
        for r in range(8, STAMP, 8):
            total = total + value[r : r + 8]
        return total

    for j in range(pairs):
        at_x = row + pair_of(offset_ref, 0, 0, 0)(j)
        at_y = column1 + pair_of(offset_ref, 1, 0, 0)(j)
        inside = (at_x >= 0) & (at_x < tile) & (at_y >= 0) & (at_y < tile)
        own = slice(128 * j, 128 * (j + 1))
        masked = [jnp.where(inside, blurred[k, :, own], 0.0) for k in range(3)]
        for k in range(3):
            blurred[k, :, own] = masked[k]
        n = 0
        for k in range(3):
            for l in range(k, 3):
                partial[8 * n : 8 * (n + 1), own] = fold(masked[k] * masked[l])
                n += 1

    segment = jnp.where(
        jnp.right_shift(lax.broadcasted_iota(jnp.int32, (slots * STAMP, 128), 0), 6)
        == lax.broadcasted_iota(jnp.int32, (slots * STAMP, 128), 1),
        1.0,
        0.0,
    ).astype(BF16)

    def gather_sums(value):
        high, low = split(value)
        out = jnp.dot(high, segment, preferred_element_type=F32)
        out = out + jnp.dot(low, segment, preferred_element_type=F32)
        return jnp.concatenate(
            [
                jnp.sum(out[8 * k : 8 * (k + 1)], axis=0, keepdims=True)
                for k in range(value.shape[0] // 8)
            ],
            axis=0,
        )

    normal = gather_sums(partial[0:48, :])

    apart = lax.broadcasted_iota(jnp.int32, (STAMP, tile), 1) - lax.broadcasted_iota(
        jnp.int32, (STAMP, tile), 0
    )
    pick = jnp.concatenate(
        [
            jnp.where(apart == offset_ref[0, 0, 0, s], 1.0, 0.0).astype(BF16)
            for s in range(slots)
        ],
        axis=0,
    )

    fetch_image.wait()
    opposite = [1, 0, 3, 2, 7, 6, 5, 4]
    for d in range(8):

        @pl.when(exists[opposite[d]] == 1)
        def _():
            halos[d].wait_recv()

    ones = jnp.ones((1, 128), jnp.int32)
    has_up, has_down, has_left, has_right = [
        ones * there > 0 for there in (above, below, before, after)
    ]
    low_lanes = lane1 < MARGIN
    high_lanes = lane1 >= 128 - MARGIN

    def unpack(block, c, first_lane):
        turn = (first_lane + 128 - 32 * c) % 128
        return pltpu.roll(block, turn, 1) if turn else block

    def unpack_corner(block, first_lane):
        return jnp.concatenate([unpack(block, c, first_lane) for c in range(4)], axis=0)

    for c in range(4):
        for g in range(2):
            r0 = 64 * c
            own = slice(128 * g, 128 * (g + 1))
            total = canvas[MARGIN + r0 : MARGIN + r0 + 64, own]
            if g == 0:
                total = total + jnp.where(low_lanes & has_left, unpack(in_sides[1], c, 0), 0.0)
            else:
                total = total + jnp.where(high_lanes & has_right, unpack(in_sides[0], c, 96), 0.0)
            if c == 0:
                edge = jnp.where(has_up, in_rows[1, :, own], 0.0)
                if g == 0:
                    corner, there = unpack_corner(in_corners[3], 0), low_lanes & has_up & has_left
                else:
                    corner, there = unpack_corner(in_corners[2], 96), high_lanes & has_up & has_right
                edge = edge + jnp.where(there, corner, 0.0)
                total = jnp.concatenate([total[0:32] + edge, total[32:64]], axis=0)
            if c == 3:
                edge = jnp.where(has_down, in_rows[0, :, own], 0.0)
                if g == 0:
                    corner, there = unpack_corner(in_corners[1], 0), low_lanes & has_down & has_left
                else:
                    corner, there = unpack_corner(in_corners[0], 96), high_lanes & has_down & has_right
                edge = edge + jnp.where(there, corner, 0.0)
                total = jnp.concatenate([total[0:32], total[32:64] + edge], axis=0)
            remain_ref[0, r0 : r0 + 64, own] = image[r0 : r0 + 64, own] - total

    high, low = split(remain_ref[0])
    strips = jnp.dot(pick, high, preferred_element_type=F32)
    strips = strips + jnp.dot(pick, low, preferred_element_type=F32)
    for j in range(pairs):
        halves = []
        for odd in range(2):
            s = 2 * j + odd
            at_y = offset_ref[1, 0, 0, s]
            turn = jnp.bitwise_and(at_y, 127)
            block = jnp.right_shift(at_y - turn, 7)
            strip = strips[STAMP * s : STAMP * (s + 1)]
            take_one = jnp.where(lane1 >= turn, block, block + 1) >= 1
            value = jnp.where(take_one, strip[:, 128:256], strip[:, 0:128])
            halves.append(
                pltpu.roll(value, jnp.bitwise_and(STAMP * odd + 256 - turn, 127), 1)
            )
        cutout = jnp.where(first_half, halves[0], halves[1])
        own = slice(128 * j, 128 * (j + 1))
        for k in range(3):
            partial[48 + 8 * k : 56 + 8 * k, own] = fold(blurred[k, :, own] * cutout)
    rights = gather_sums(partial[48:72, :])
    weight = weight_ref[0]
    sums[me] = weight * jnp.concatenate([normal, rights, jnp.zeros((7, 128), F32)], axis=0)

    shares = []
    for d in range(1, nb):
        share = pltpu.make_async_remote_copy(
            src_ref=sums.at[me],
            dst_ref=sums.at[me],
            send_sem=sum_send.at[d - 1],
            recv_sem=sum_recv.at[d - 1],
            device_id=peers[d - 1],
            device_id_type=MESH,
        )
        share.start()
        shares.append(share)
    for d in range(1, nb):
        source = lax.rem(me + nb - d, nb)
        pltpu.make_async_remote_copy(
            src_ref=sums.at[source],
            dst_ref=sums.at[source],
            send_sem=sum_send.at[d - 1],
            recv_sem=sum_recv.at[d - 1],
            device_id=peers[d - 1],
            device_id_type=MESH,
        ).wait_recv()
    total = sums[0]
    for e in range(1, nb):
        total = total + sums[e]
    sums_ref[...] = total
    sums_ref[9:10, 0:slots] = flux_vec[0]
    sums_ref[10:11, 0:slots] = shift_vec[0, 0]
    sums_ref[11:12, 0:slots] = shift_vec[1, 0]
    sums_ref[12:13, :] = jnp.where(lane1 < live_count, 1.0, 0.0)

    for share in shares:
        share.wait_send()
    for halo, there in zip(halos, exists):

        @pl.when(there == 1)
        def _():
            halo.wait_send()


def finish(sums_ref, remain_ref, refined_hbm, residual_hbm, refined, sems):
    store = pltpu.make_async_copy(remain_ref, residual_hbm, sems.at[0])
    store.start()
    slots = refined.shape[3]
    entry = [sums_ref[n : n + 1, 0:slots] for n in range(13)]
    start, live = entry[9], entry[12]
    flux = start * live
    m01, m02 = entry[1] * flux, entry[2] * flux
    m12 = entry[4] * flux * flux
    m00 = entry[0] + PRIOR
    m11 = entry[3] * flux * flux + PRIOR
    m22 = entry[5] * flux * flux + PRIOR
    v0, v1, v2 = entry[6], entry[7] * flux, entry[8] * flux
    c00 = m11 * m22 - m12 * m12
    c01 = m12 * m02 - m01 * m22
    c02 = m01 * m12 - m11 * m02
    c11 = m00 * m22 - m02 * m02
    c12 = m01 * m02 - m00 * m12
    c22 = m00 * m11 - m01 * m01
    determinant = m00 * c00 + m01 * c01 + m02 * c02
    change = [
        (c00 * v0 + c01 * v1 + c02 * v2) / determinant,
        (c01 * v0 + c11 * v1 + c12 * v2) / determinant,
        (c02 * v0 + c12 * v1 + c22 * v2) / determinant,
    ]
    for k in range(3):
        refined[k, 0] = (entry[9 + k] + change[k]) * live
    write = pltpu.make_async_copy(refined, refined_hbm, sems.at[1])
    write.start()
    store.wait()
    write.wait()


def shards(
    image,
    psf_taps,
    exposure_weight,
    flux_start,
    centre_shift,
    radius,
    ellipticity,
    offsets,
    source_count,
):
    tile = image.shape[1]
    slots = flux_start.shape[2]
    rows = tile + 2 * MARGIN
    width = slots * STAMP
    vmem = pl.BlockSpec(memory_space=pltpu.VMEM)
    hbm = pl.BlockSpec(memory_space=pl.ANY)
    peers = lax.axis_size("be") - 1
    operands = (
        psf_taps,
        exposure_weight,
        flux_start,
        centre_shift,
        radius,
        ellipticity,
        offsets,
        source_count,
    )
    sums, remain = pl.pallas_call(
        kernel,
        out_shape=(pltpu.VMEM((16, 128), F32), pltpu.VMEM(image.shape, F32)),
        in_specs=[hbm] * 9,
        out_specs=(vmem, vmem),
        scratch_shapes=[pltpu.SMEM(operand.shape, operand.dtype) for operand in operands]
        + [
            pltpu.VMEM(flux_start.shape, F32),
            pltpu.VMEM(centre_shift.shape, F32),
            pltpu.VMEM((tile, tile), F32),
            pltpu.VMEM((3 * STAMP, 2 * width), BF16),
            pltpu.VMEM((2, STAMP, width), F32),
            pltpu.VMEM((3, STAMP, width), F32),
            pltpu.VMEM((width, tile + 128), BF16),
            pltpu.VMEM((width, tile + 128), BF16),
            pltpu.VMEM((rows, tile + 128), F32),
            pltpu.VMEM((2, STAMP, 128), F32),
            pltpu.VMEM((4, 8, 128), F32),
            pltpu.VMEM((2, MARGIN, tile), F32),
            pltpu.VMEM((2, STAMP, 128), F32),
            pltpu.VMEM((4, 8, 128), F32),
            pltpu.VMEM((72, width), F32),
            pltpu.VMEM((peers + 1, 16, 128), F32),
            pltpu.SemaphoreType.DMA((11,)),
            pltpu.SemaphoreType.DMA((8,)),
            pltpu.SemaphoreType.DMA((8,)),
            pltpu.SemaphoreType.DMA((peers,)),
            pltpu.SemaphoreType.DMA((peers,)),
        ],
        compiler_params=pltpu.CompilerParams(collective_id=0, has_side_effects=True),
        name="photometry",
    )(image, *operands)
    sums = pltpu.with_memory_space_constraint(sums, pltpu.VMEM)
    remain = pltpu.with_memory_space_constraint(remain, pltpu.VMEM)
    return pl.pallas_call(
        finish,
        out_shape=(
            jax.ShapeDtypeStruct((3, 1, 1, slots), F32),
            jax.ShapeDtypeStruct(image.shape, F32),
        ),
        in_specs=[vmem, vmem],
        out_specs=(hbm, hbm),
        scratch_shapes=[pltpu.VMEM((3, 1, 1, slots), F32), pltpu.SemaphoreType.DMA((2,))],
        name="finish",
    )(sums, remain)


def solution(mesh):
    return jax.shard_map(
        shards,
        mesh=mesh,
        in_specs=(
            P("be", "skyx", "skyy"),
            P("be", None, None),
            P("be"),
            P("skyx", "skyy", None),
            P(None, "skyx", "skyy", None),
            P("skyx", "skyy", None),
            P(None, "skyx", "skyy", None),
            P(None, "skyx", "skyy", None),
            P("skyx", "skyy"),
        ),
        out_specs=(P(None, "skyx", "skyy", None), P("be", "skyx", "skyy")),
        check_vma=False,
    )
```

```python
import jax
import jax.numpy as jnp
from jax import lax
from jax.experimental import pallas as pl
from jax.experimental.pallas import tpu as pltpu
from jax.sharding import PartitionSpec as P

STAMP = 64
MARGIN = 32
TAPS = 15
PRIOR = 8.0
EDGES = 4
F32 = jnp.float32
BF16 = jnp.bfloat16
MESH = pl.DeviceIdType.MESH


def split(x):
    high = x.astype(BF16)
    return high, (x - high.astype(F32)).astype(BF16)


def band(taps_ref, which, differ):
    total = taps_ref[0, which, 0]
    for t in range(1, TAPS):
        total = total + taps_ref[0, which, t]
    out = jnp.zeros(differ.shape, F32)
    for t in range(TAPS):
        out = jnp.where(differ == t - TAPS // 2, taps_ref[0, which, t], out)
    return out / jnp.full(differ.shape, total, F32)


def kernel(
    image_hbm,
    taps_hbm,
    weight_hbm,
    flux_hbm,
    shift_hbm,
    radius_hbm,
    ellipse_hbm,
    offset_hbm,
    count_hbm,
    sums_ref,
    remain_ref,
    taps_ref,
    weight_ref,
    flux_ref,
    shift_ref,
    radius_ref,
    ellipse_ref,
    offset_ref,
    count_ref,
    flux_vec,
    shift_vec,
    image,
    edge_stacked,
    edge_lanes,
    edge_rows,
    pack_sides,
    pack_corners,
    in_rows,
    in_sides,
    in_corners,
    stacked,
    blurred,
    lanes,
    blocks,
    partial,
    sums,
    copy_sems,
    send_sems,
    recv_sems,
    sum_send,
    sum_recv,
):
    slots = flux_hbm.shape[2]
    tile = image_hbm.shape[1]
    pairs = slots // 2
    mx = lax.axis_index("skyx")
    my = lax.axis_index("skyy")
    me = lax.axis_index("be")
    nx = lax.axis_size("skyx")
    ny = lax.axis_size("skyy")
    nb = lax.axis_size("be")
    above, below = (mx > 0).astype(jnp.int32), (mx < nx - 1).astype(jnp.int32)
    before, after = (my > 0).astype(jnp.int32), (my < ny - 1).astype(jnp.int32)
    around = [
        (mx, my - before, me),
        (mx, my + after, me),
        (mx - above, my - before, me),
        (mx - above, my + after, me),
        (mx + below, my - before, me),
        (mx + below, my + after, me),
        (mx - above, my, me),
        (mx + below, my, me),
    ]
    exists = [
        before,
        after,
        above * before,
        above * after,
        below * before,
        below * after,
        above,
        below,
    ]
    opposite = [1, 0, 5, 4, 3, 2, 7, 6]
    peers = [(mx, my, lax.rem(me + d, nb)) for d in range(1, nb)]

    barrier = pltpu.get_barrier_semaphore()
    for device, there in zip(around, exists):

        @pl.when(there == 1)
        def _():
            pl.semaphore_signal(barrier, inc=1, device_id=device, device_id_type=MESH)

    for device in peers:
        pl.semaphore_signal(barrier, inc=1, device_id=device, device_id_type=MESH)

    small = [
        (offset_hbm, offset_ref),
        (count_hbm, count_ref),
        (shift_hbm, shift_ref),
        (radius_hbm, radius_ref),
        (ellipse_hbm, ellipse_ref),
        (flux_hbm, flux_ref),
        (taps_hbm, taps_ref),
        (weight_hbm, weight_ref),
        (flux_hbm, flux_vec),
        (shift_hbm, shift_vec),
    ]
    fetches = [
        pltpu.make_async_copy(source, target, copy_sems.at[n + 1])
        for n, (source, target) in enumerate(small)
    ]
    for fetch in fetches:
        fetch.start()
    fetch_image = pltpu.make_async_copy(image_hbm.at[0], image, copy_sems.at[0])
    fetch_image.start()
    for fetch in fetches:
        fetch.wait()

    row = lax.broadcasted_iota(jnp.int32, (STAMP, 128), 0)
    lane = lax.broadcasted_iota(jnp.int32, (STAMP, 128), 1)
    lane1 = lax.broadcasted_iota(jnp.int32, (1, 128), 1)
    lane16 = lax.broadcasted_iota(jnp.int32, (16, 128), 1)
    first_half = lane1 < STAMP
    column1 = jnp.where(first_half, lane1, lane1 - STAMP)
    grid_u = row.astype(F32)
    grid_v = column1.astype(F32)
    live_count = count_ref[0, 0]

    def pair_of(j, ref, *index):
        return jnp.where(first_half, ref[index + (2 * j,)], ref[index + (2 * j + 1,)])

    rows_band = band(taps_ref, 0, row[:, :STAMP] - lane[:, :STAMP])
    rows_high, rows_low = split(rows_band)
    left_factor = jnp.concatenate([rows_high, rows_high, rows_low], axis=1)
    columns_band = jnp.where(lane < STAMP, band(taps_ref, 1, lane - row), 0.0)
    columns_next = pltpu.roll(columns_band, STAMP, 1)
    nothing = jnp.zeros((STAMP, 128), F32)
    right_factor = jnp.concatenate(
        [
            jnp.concatenate([columns_band, nothing], axis=1),
            jnp.concatenate([columns_next, nothing], axis=1),
            jnp.concatenate([nothing, columns_band], axis=1),
            jnp.concatenate([nothing, columns_next], axis=1),
        ],
        axis=0,
    )
    right_high, right_low = split(right_factor)

    def blur(ref, width):
        along = jnp.dot(left_factor, ref[:, :width], preferred_element_type=F32)
        groups = jnp.concatenate(
            [along[:, 256 * g : 256 * (g + 1)] for g in range(width // 256)], axis=0
        )
        high, low = split(groups)
        out = jnp.dot(high, right_high, preferred_element_type=F32)
        out = out + jnp.dot(low, right_high, preferred_element_type=F32)
        return out + jnp.dot(high, right_low, preferred_element_type=F32)

    def stack(ref, value, start):
        high, low = split(value)
        ref[0:STAMP, start : start + 128] = high
        ref[STAMP : 2 * STAMP, start : start + 128] = low
        ref[2 * STAMP : 3 * STAMP, start : start + 128] = high

    def shape(shift_x, shift_y, radius, one, two):
        inverse = 1.0 / (radius * radius)
        coef_a = (1.0 + one) * inverse
        coef_b = two * inverse
        coef_c = (1.0 - one) * inverse
        u = grid_u - (float(STAMP // 2) + shift_x)
        v = grid_v - (float(STAMP // 2) + shift_y)
        along_x = coef_a * u + coef_b * v
        along_y = coef_b * u + coef_c * v
        square = u * along_x + v * along_y + 0.25
        inverse_root = lax.rsqrt(square)
        profile = jnp.exp(-(square * inverse_root))
        return profile, profile * inverse_root, along_x, along_y

    def lane_place(both, odd, at_y, groups, write):
        turn = jnp.bitwise_and(at_y, 127)
        block = jnp.right_shift(at_y - turn, 7)
        value = pltpu.roll(both, jnp.bitwise_and(turn + 128 - STAMP * odd, 127), 1)
        high, low = split(value)
        owner = jnp.where(lane16 >= turn, block, block + 1)
        owner = jnp.where(owner == -1, 2, owner)
        owner = jnp.where(jnp.bitwise_and(lane16 - turn, 127) < STAMP, owner, 3)
        for g in range(groups):
            keep = jnp.where(owner == g, 1.0, 0.0).astype(BF16)
            for r in range(0, STAMP, 16):
                write(g, 0, r, high[r : r + 16] * keep)
                write(g, 1, r, low[r : r + 16] * keep)

    keys, found = [], jnp.int32(0)
    edge_y = [jnp.int32(0)] * EDGES
    last = tile - STAMP
    for s in range(slots):
        at_x, at_y = offset_ref[0, 0, 0, s], offset_ref[1, 0, 0, s]
        reach = jnp.maximum(jnp.maximum(-at_x, at_x - last), jnp.maximum(-at_y, at_y - last))
        hit = jnp.where(s < live_count, reach, 0) > 0
        key = jnp.where(hit, found, -1)
        found = jnp.where(hit, found + 1, found)
        keys.append(key)
        edge_y = [jnp.where(key == k, at_y, edge_y[k]) for k in range(EDGES)]
    edge = []
    for h in range(EDGES // 2):
        which = jnp.where(first_half, 2 * h, 2 * h + 1)
        values = [jnp.full((1, 128), v, F32) for v in (0.0, 0.0, 1.0, 0.0, 0.0, 0.0)]
        values.append(jnp.zeros((1, 128), jnp.int32))
        for s in range(slots):
            here = which == keys[s]
            new = [
                shift_ref[0, 0, 0, s],
                shift_ref[1, 0, 0, s],
                radius_ref[0, 0, s],
                ellipse_ref[0, 0, 0, s],
                ellipse_ref[1, 0, 0, s],
                flux_ref[0, 0, s],
                offset_ref[0, 0, 0, s],
            ]
            values = [jnp.where(here, n, v) for n, v in zip(new, values)]
        edge.append(values)
        stack(edge_stacked, shape(*values[:5])[0], 128 * h)
    spread = blur(edge_stacked, STAMP * EDGES)
    for k in range(EDGES):
        both = spread[:, 128 * (k // 2) : 128 * (k // 2 + 1)] * edge[k // 2][5]

        def write(g, part, r, value):
            start = 256 * part + 128 * g if g < 2 else 512 + 128 * part
            edge_lanes[STAMP * k + r : STAMP * k + r + 16, start : start + 128] = value

        lane_place(both, k % 2, edge_y[k], 3, write)
    edge_target = jnp.concatenate([values[6] + column1 for values in edge], axis=1)
    at = lax.broadcasted_iota(jnp.int32, (2 * MARGIN, STAMP * EDGES), 0)
    at = jnp.where(at < MARGIN, at - MARGIN, at - MARGIN + tile)
    place = jnp.where(at == edge_target, 1.0, 0.0).astype(BF16)
    outer = jnp.dot(place, edge_lanes[...], preferred_element_type=F32)
    at = lax.broadcasted_iota(jnp.int32, (tile, STAMP * EDGES), 0)
    place = jnp.where(at == edge_target, 1.0, 0.0).astype(BF16)
    side = jnp.dot(place, edge_lanes[:, 512:768], preferred_element_type=F32)
    side = side[:, 0:128] + side[:, 128:256]
    corners = outer[:, 512:640] + outer[:, 640:768]

    def pack(strip, first_lane):
        size = strip.shape[0] // 4
        place_in = lax.broadcasted_iota(jnp.int32, (size, 128), 1)
        out = None
        for c in range(4):
            turn = (32 * c + 128 - first_lane) % 128
            block = strip[size * c : size * (c + 1)]
            block = pltpu.roll(block, turn, 1) if turn else block
            out = block if c == 0 else jnp.where(place_in >= 32 * c, block, out)
        return out

    for p in range(2):
        strip = corners[MARGIN * p : MARGIN * (p + 1)]
        edge_rows[p] = outer[MARGIN * p : MARGIN * (p + 1), 0:256] + (
            outer[MARGIN * p : MARGIN * (p + 1), 256:512]
        )
        pack_sides[p] = pack(side, 96 - 96 * p)
        pack_corners[2 * p] = pack(strip, 96)
        pack_corners[2 * p + 1] = pack(strip, 0)

    sources = [pack_sides.at[d] for d in range(2)] + [pack_corners.at[d] for d in range(4)]
    sources += [edge_rows.at[d] for d in range(2)]
    landings = [in_sides.at[d] for d in range(2)] + [in_corners.at[d] for d in range(4)]
    landings += [in_rows.at[d] for d in range(2)]
    pl.semaphore_wait(barrier, len(peers) + sum(exists))
    halos = [
        pltpu.make_async_remote_copy(
            src_ref=sources[d],
            dst_ref=landings[d],
            send_sem=send_sems.at[d],
            recv_sem=recv_sems.at[d],
            device_id=around[d],
            device_id_type=MESH,
        )
        for d in range(8)
    ]
    for halo, there in zip(halos, exists):

        @pl.when(there == 1)
        def _():
            halo.start()

    for j in range(pairs):
        profile, scaled, along_x, along_y = shape(
            pair_of(j, shift_ref, 0, 0, 0),
            pair_of(j, shift_ref, 1, 0, 0),
            pair_of(j, radius_ref, 0, 0),
            pair_of(j, ellipse_ref, 0, 0, 0),
            pair_of(j, ellipse_ref, 1, 0, 0),
        )
        stack(stacked, profile, 128 * j)
        stack(stacked, scaled * along_x, STAMP * slots + 128 * j)
        stack(stacked, scaled * along_y, 2 * STAMP * slots + 128 * j)
    spread = blur(stacked, 3 * STAMP * slots)
    quads = slots // 4
    for k in range(3):
        for g in range(quads):
            start = STAMP * (quads * k + g)
            blurred[k, :, 256 * g : 256 * (g + 1)] = spread[start : start + STAMP]

    targets = []
    for j in range(pairs):
        slot = jnp.where(first_half, 2 * j, 2 * j + 1)
        flux = jnp.where(slot < live_count, pair_of(j, flux_ref, 0, 0), 0.0)
        both = blurred[0, :, 128 * j : 128 * (j + 1)] * flux
        for odd in range(2):
            s = 2 * j + odd

            def write(g, part, r, value):
                start = 256 * part + 128 * g
                lanes[STAMP * s + r : STAMP * s + r + 16, start : start + 128] = value

            lane_place(both, odd, offset_ref[1, 0, 0, s], 2, write)
        targets.append(pair_of(j, offset_ref, 0, 0, 0) + column1)
    target = jnp.concatenate(targets, axis=1)
    at = lax.broadcasted_iota(jnp.int32, (tile, slots * STAMP), 0)
    place = jnp.where(at == target, 1.0, 0.0).astype(BF16)
    placed = jnp.dot(place, lanes[...], preferred_element_type=F32)
    fetch_image.wait()
    remain_ref[0] = image[...] - (placed[:, :256] + placed[:, 256:])

    def fold(value):
        total = value[0:8]
        for r in range(8, STAMP, 8):
            total = total + value[r : r + 8]
        return total

    for j in range(pairs):
        at_x = row + pair_of(j, offset_ref, 0, 0, 0)
        at_y = column1 + pair_of(j, offset_ref, 1, 0, 0)
        inside = (at_x >= 0) & (at_x < tile) & (at_y >= 0) & (at_y < tile)
        own = slice(128 * j, 128 * (j + 1))
        masked = [jnp.where(inside, blurred[k, :, own], 0.0) for k in range(3)]
        for k in range(3):
            blurred[k, :, own] = masked[k]
        n = 0
        for k in range(3):
            for l in range(k, 3):
                partial[8 * n : 8 * (n + 1), own] = fold(masked[k] * masked[l])
                n += 1

    segment = jnp.where(
        jnp.right_shift(lax.broadcasted_iota(jnp.int32, (slots * STAMP, 128), 0), 6)
        == lax.broadcasted_iota(jnp.int32, (slots * STAMP, 128), 1),
        1.0,
        0.0,
    ).astype(BF16)

    def gather_sums(value):
        high, low = split(value)
        out = jnp.dot(high, segment, preferred_element_type=F32)
        out = out + jnp.dot(low, segment, preferred_element_type=F32)
        return jnp.concatenate(
            [
                jnp.sum(out[8 * k : 8 * (k + 1)], axis=0, keepdims=True)
                for k in range(value.shape[0] // 8)
            ],
            axis=0,
        )

    normal = gather_sums(partial[0:48, :])

    for r in range(MARGIN // 8):
        for g in range(2):
            blocks[r, g] = jnp.zeros((8, 128), F32)
            blocks[tile // 8 + MARGIN // 8 + r, g] = jnp.zeros((8, 128), F32)

    for d in range(8):

        @pl.when(exists[opposite[d]] == 1)
        def _():
            halos[d].wait_recv()

    ones = jnp.ones((1, 128), jnp.int32)
    has_up, has_down, has_left, has_right = [
        ones * there > 0 for there in (above, below, before, after)
    ]
    low_lanes = lane1 < MARGIN
    high_lanes = lane1 >= 128 - MARGIN

    def unpack(block, c, first_lane):
        turn = (first_lane + 128 - 32 * c) % 128
        return pltpu.roll(block, turn, 1) if turn else block

    def unpack_corner(block, first_lane):
        return jnp.concatenate([unpack(block, c, first_lane) for c in range(4)], axis=0)

    for c in range(4):
        for g in range(2):
            r0 = 64 * c
            own = slice(128 * g, 128 * (g + 1))
            if g == 0:
                total = jnp.where(low_lanes & has_left, unpack(in_sides[1], c, 0), 0.0)
            else:
                total = jnp.where(high_lanes & has_right, unpack(in_sides[0], c, 96), 0.0)
            if c == 0 or c == 3:
                there = has_up if c == 0 else has_down
                fringe = jnp.where(there, in_rows[1 if c == 0 else 0, :, own], 0.0)
                n = (3 if c == 0 else 1) - g
                corner = unpack_corner(in_corners[n], 96 * g)
                there = there & ((low_lanes & has_left) if g == 0 else (high_lanes & has_right))
                fringe = fringe + jnp.where(there, corner, 0.0)
                if c == 0:
                    total = jnp.concatenate([total[0:32] + fringe, total[32:64]], axis=0)
                else:
                    total = jnp.concatenate([total[0:32], total[32:64] + fringe], axis=0)
            value = remain_ref[0, r0 : r0 + 64, own] - total
            remain_ref[0, r0 : r0 + 64, own] = value
            for r in range(8):
                blocks[MARGIN // 8 + 8 * c + r, g] = value[8 * r : 8 * (r + 1)]

    sub = lax.broadcasted_iota(jnp.int32, (STAMP // 8, 8, 128), 1)
    for j in range(pairs):
        halves = []
        for odd in range(2):
            s = 2 * j + odd
            at_x = jnp.clip(offset_ref[0, 0, 0, s] + MARGIN, 0, tile - 1)
            step = jnp.bitwise_and(at_x, 7)
            first = jnp.right_shift(at_x, 3)
            at_y = offset_ref[1, 0, 0, s]
            turn = jnp.bitwise_and(at_y, 127)
            block = jnp.right_shift(at_y - turn, 7)
            take_one = jnp.where(lane1 >= turn, block, block + 1) >= 1
            value = jnp.stack(
                [
                    jnp.where(take_one, blocks[first + r, 1], blocks[first + r, 0])
                    for r in range(STAMP // 8 + 1)
                ]
            )
            value = pltpu.roll(value, jnp.bitwise_and(STAMP * odd + 256 - turn, 127), 2)
            value = pltpu.roll(value, jnp.bitwise_and(8 - step, 7), 1)
            value = jnp.where(sub < 8 - step, value[:-1], value[1:])
            halves.append(value.reshape(STAMP, 128))
        cutout = jnp.where(first_half, halves[0], halves[1])
        own = slice(128 * j, 128 * (j + 1))
        for k in range(3):
            partial[48 + 8 * k : 56 + 8 * k, own] = fold(blurred[k, :, own] * cutout)
    rights = gather_sums(partial[48:72, :])
    weight = weight_ref[0]
    sums[me] = weight * jnp.concatenate([normal, rights, jnp.zeros((7, 128), F32)], axis=0)

    shares = []
    for d in range(1, nb):
        share = pltpu.make_async_remote_copy(
            src_ref=sums.at[me],
            dst_ref=sums.at[me],
            send_sem=sum_send.at[d - 1],
            recv_sem=sum_recv.at[d - 1],
            device_id=peers[d - 1],
            device_id_type=MESH,
        )
        share.start()
        shares.append(share)
    for d in range(1, nb):
        source = lax.rem(me + nb - d, nb)
        pltpu.make_async_remote_copy(
            src_ref=sums.at[source],
            dst_ref=sums.at[source],
            send_sem=sum_send.at[d - 1],
            recv_sem=sum_recv.at[d - 1],
            device_id=peers[d - 1],
            device_id_type=MESH,
        ).wait_recv()
    total = sums[0]
    for e in range(1, nb):
        total = total + sums[e]
    sums_ref[...] = total
    sums_ref[9:10, 0:slots] = flux_vec[0]
    sums_ref[10:11, 0:slots] = shift_vec[0, 0]
    sums_ref[11:12, 0:slots] = shift_vec[1, 0]
    sums_ref[12:13, :] = jnp.where(lane1 < live_count, 1.0, 0.0)

    for share in shares:
        share.wait_send()
    for halo, there in zip(halos, exists):

        @pl.when(there == 1)
        def _():
            halo.wait_send()


def finish(sums_ref, remain_ref, refined_hbm, residual_hbm, refined, sems):
    store = pltpu.make_async_copy(remain_ref, residual_hbm, sems.at[0])
    store.start()
    slots = refined.shape[3]
    entry = [sums_ref[n : n + 1, 0:slots] for n in range(13)]
    start, live = entry[9], entry[12]
    flux = start * live
    m01, m02 = entry[1] * flux, entry[2] * flux
    m12 = entry[4] * flux * flux
    m00 = entry[0] + PRIOR
    m11 = entry[3] * flux * flux + PRIOR
    m22 = entry[5] * flux * flux + PRIOR
    v0, v1, v2 = entry[6], entry[7] * flux, entry[8] * flux
    c00 = m11 * m22 - m12 * m12
    c01 = m12 * m02 - m01 * m22
    c02 = m01 * m12 - m11 * m02
    c11 = m00 * m22 - m02 * m02
    c12 = m01 * m02 - m00 * m12
    c22 = m00 * m11 - m01 * m01
    determinant = m00 * c00 + m01 * c01 + m02 * c02
    change = [
        (c00 * v0 + c01 * v1 + c02 * v2) / determinant,
        (c01 * v0 + c11 * v1 + c12 * v2) / determinant,
        (c02 * v0 + c12 * v1 + c22 * v2) / determinant,
    ]
    for k in range(3):
        refined[k, 0] = (entry[9 + k] + change[k]) * live
    write = pltpu.make_async_copy(refined, refined_hbm, sems.at[1])
    write.start()
    store.wait()
    write.wait()


def shards(
    image,
    psf_taps,
    exposure_weight,
    flux_start,
    centre_shift,
    radius,
    ellipticity,
    offsets,
    source_count,
):
    tile = image.shape[1]
    slots = flux_start.shape[2]
    rows = tile + 2 * MARGIN
    width = slots * STAMP
    vmem = pl.BlockSpec(memory_space=pltpu.VMEM)
    hbm = pl.BlockSpec(memory_space=pl.ANY)
    peers = lax.axis_size("be") - 1
    operands = (
        psf_taps,
        exposure_weight,
        flux_start,
        centre_shift,
        radius,
        ellipticity,
        offsets,
        source_count,
    )
    sums, remain = pl.pallas_call(
        kernel,
        out_shape=(pltpu.VMEM((16, 128), F32), pltpu.VMEM(image.shape, F32)),
        in_specs=[hbm] * 9,
        out_specs=(vmem, vmem),
        scratch_shapes=[pltpu.SMEM(operand.shape, operand.dtype) for operand in operands]
        + [
            pltpu.VMEM(flux_start.shape, F32),
            pltpu.VMEM(centre_shift.shape, F32),
            pltpu.VMEM((tile, tile), F32),
            pltpu.VMEM((3 * STAMP, EDGES * STAMP), BF16),
            pltpu.VMEM((EDGES * STAMP, 768), BF16),
            pltpu.VMEM((2, MARGIN, tile), F32),
            pltpu.VMEM((2, STAMP, 128), F32),
            pltpu.VMEM((4, 8, 128), F32),
            pltpu.VMEM((2, MARGIN, tile), F32),
            pltpu.VMEM((2, STAMP, 128), F32),
            pltpu.VMEM((4, 8, 128), F32),
            pltpu.VMEM((3 * STAMP, 3 * width), BF16),
            pltpu.VMEM((3, STAMP, width), F32),
            pltpu.VMEM((width, 2 * tile), BF16),
            pltpu.VMEM((rows // 8, 2, 8, 128), F32),
            pltpu.VMEM((72, width), F32),
            pltpu.VMEM((peers + 1, 16, 128), F32),
            pltpu.SemaphoreType.DMA((11,)),
            pltpu.SemaphoreType.DMA((8,)),
            pltpu.SemaphoreType.DMA((8,)),
            pltpu.SemaphoreType.DMA((peers,)),
            pltpu.SemaphoreType.DMA((peers,)),
        ],
        compiler_params=pltpu.CompilerParams(collective_id=0, has_side_effects=True),
        name="photometry",
    )(image, *operands)
    sums = pltpu.with_memory_space_constraint(sums, pltpu.VMEM)
    remain = pltpu.with_memory_space_constraint(remain, pltpu.VMEM)
    return pl.pallas_call(
        finish,
        out_shape=(
            jax.ShapeDtypeStruct((3, 1, 1, slots), F32),
            jax.ShapeDtypeStruct(image.shape, F32),
        ),
        in_specs=[vmem, vmem],
        out_specs=(hbm, hbm),
        scratch_shapes=[pltpu.VMEM((3, 1, 1, slots), F32), pltpu.SemaphoreType.DMA((2,))],
        name="finish",
    )(sums, remain)


def solution(mesh):
    return jax.shard_map(
        shards,
        mesh=mesh,
        in_specs=(
            P("be", "skyx", "skyy"),
            P("be", None, None),
            P("be"),
            P("skyx", "skyy", None),
            P(None, "skyx", "skyy", None),
            P("skyx", "skyy", None),
            P(None, "skyx", "skyy", None),
            P(None, "skyx", "skyy", None),
            P("skyx", "skyy"),
        ),
        out_specs=(P(None, "skyx", "skyy", None), P("be", "skyx", "skyy")),
        check_vma=False,
    )
```

```python
import jax
import jax.numpy as jnp
from jax import lax
from jax.experimental import pallas as pl
from jax.experimental.pallas import tpu as pltpu
from jax.sharding import PartitionSpec as P

STAMP = 64
MARGIN = 32
TAPS = 15
PRIOR = 8.0
EDGES = 4
F32 = jnp.float32
BF16 = jnp.bfloat16
MESH = pl.DeviceIdType.MESH


def split(x):
    high = x.astype(BF16)
    return high, (x - high.astype(F32)).astype(BF16)


def band(taps_ref, which, differ):
    total = taps_ref[0, which, 0]
    for t in range(1, TAPS):
        total = total + taps_ref[0, which, t]
    out = jnp.zeros(differ.shape, F32)
    for t in range(TAPS):
        out = jnp.where(differ == t - TAPS // 2, taps_ref[0, which, t], out)
    return out / jnp.full(differ.shape, total, F32)


def kernel(
    image_hbm,
    taps_hbm,
    weight_ref,
    flux_hbm,
    shift_hbm,
    radius_hbm,
    ellipse_hbm,
    offset_hbm,
    count_ref,
    sums_ref,
    remain_ref,
    taps_ref,
    flux_ref,
    shift_ref,
    radius_ref,
    ellipse_ref,
    offset_ref,
    flux_vec,
    shift_vec,
    image,
    edge_lanes,
    edge_rows,
    pack_sides,
    pack_corners,
    in_rows,
    in_sides,
    in_corners,
    stacked,
    blurred,
    lanes,
    blocks,
    partial,
    normals,
    rights,
    copy_sems,
    send_sems,
    recv_sems,
    normal_send,
    normal_recv,
    right_send,
    right_recv,
):
    slots = flux_hbm.shape[2]
    tile = image_hbm.shape[1]
    pairs = slots // 2
    mx = lax.axis_index("skyx")
    my = lax.axis_index("skyy")
    me = lax.axis_index("be")
    nx = lax.axis_size("skyx")
    ny = lax.axis_size("skyy")
    nb = lax.axis_size("be")
    above, below = (mx > 0).astype(jnp.int32), (mx < nx - 1).astype(jnp.int32)
    before, after = (my > 0).astype(jnp.int32), (my < ny - 1).astype(jnp.int32)
    around = [
        (mx, my - before, me),
        (mx, my + after, me),
        (mx - above, my - before, me),
        (mx - above, my + after, me),
        (mx + below, my - before, me),
        (mx + below, my + after, me),
        (mx - above, my, me),
        (mx + below, my, me),
    ]
    exists = [
        before,
        after,
        above * before,
        above * after,
        below * before,
        below * after,
        above,
        below,
    ]
    opposite = [1, 0, 5, 4, 3, 2, 7, 6]
    peers = [(mx, my, lax.rem(me + d, nb)) for d in range(1, nb)]

    barrier = pltpu.get_barrier_semaphore()
    for device, there in zip(around, exists):

        @pl.when(there == 1)
        def _():
            pl.semaphore_signal(barrier, inc=1, device_id=device, device_id_type=MESH)

    small = [
        (offset_hbm, offset_ref),
        (shift_hbm, shift_ref),
        (radius_hbm, radius_ref),
        (ellipse_hbm, ellipse_ref),
        (flux_hbm, flux_ref),
        (taps_hbm, taps_ref),
    ]
    late = [(image_hbm.at[0], image), (flux_hbm, flux_vec), (shift_hbm, shift_vec)]
    fetches = [
        pltpu.make_async_copy(source, target, copy_sems.at[n])
        for n, (source, target) in enumerate(small + late)
    ]
    for fetch in fetches[: len(small)]:
        fetch.start()
    for device in peers:
        pl.semaphore_signal(barrier, inc=1, device_id=device, device_id_type=MESH)
    for fetch in fetches[len(small) :]:
        fetch.start()
    for fetch in fetches[: len(small)]:
        fetch.wait()

    row = lax.broadcasted_iota(jnp.int32, (STAMP, 128), 0)
    lane = lax.broadcasted_iota(jnp.int32, (STAMP, 128), 1)
    lane1 = lax.broadcasted_iota(jnp.int32, (1, 128), 1)
    lane16 = lax.broadcasted_iota(jnp.int32, (16, 128), 1)
    first_half = lane1 < STAMP
    column1 = jnp.where(first_half, lane1, lane1 - STAMP)
    grid_u = row.astype(F32)
    grid_v = column1.astype(F32)
    live_count = count_ref[0, 0]

    def pair_of(j, ref, *index):
        return jnp.where(first_half, ref[index + (2 * j,)], ref[index + (2 * j + 1,)])

    rows_band = jnp.where(lane < STAMP, band(taps_ref, 0, row - lane), 0.0)
    columns_band = jnp.where(lane < STAMP, band(taps_ref, 1, lane - row), 0.0)
    nothing = jnp.zeros((STAMP, 128), F32)

    def diagonal(block):
        other = pltpu.roll(block, STAMP, 1)
        return jnp.concatenate(
            [
                jnp.concatenate([block, nothing], axis=1),
                jnp.concatenate([other, nothing], axis=1),
                jnp.concatenate([nothing, block], axis=1),
                jnp.concatenate([nothing, other], axis=1),
            ],
            axis=0,
        )

    right_high, right_low = split(diagonal(columns_band))
    left_high, left_low = split(diagonal(rows_band))
    rows_high, rows_low = left_high[:STAMP, :STAMP], left_low[:STAMP, :STAMP]
    left_factor = jnp.concatenate([rows_high, rows_high, rows_low], axis=1)

    def blur_columns(groups):
        size = groups.shape[0]
        high, low = split(groups)
        out = jnp.dot(
            jnp.concatenate([high, low], axis=0), right_high, preferred_element_type=F32
        )
        return out[:size] + out[size:] + jnp.dot(high, right_low, preferred_element_type=F32)

    def blur(ref, width):
        along = jnp.dot(left_factor, ref[:, :width], preferred_element_type=F32)
        groups = jnp.concatenate(
            [along[:, 256 * g : 256 * (g + 1)] for g in range(width // 256)], axis=0
        )
        return blur_columns(groups)

    def stack(ref, value, start):
        high, low = split(value)
        ref[0:STAMP, start : start + 128] = high
        ref[STAMP : 2 * STAMP, start : start + 128] = low
        ref[2 * STAMP : 3 * STAMP, start : start + 128] = high

    def shape(shift_x, shift_y, radius, one, two):
        inverse = 1.0 / (radius * radius)
        coef_a = (1.0 + one) * inverse
        coef_b = two * inverse
        coef_c = (1.0 - one) * inverse
        u = grid_u - (float(STAMP // 2) + shift_x)
        v = grid_v - (float(STAMP // 2) + shift_y)
        along_x = coef_a * u + coef_b * v
        along_y = coef_b * u + coef_c * v
        square = u * along_x + v * along_y + 0.25
        inverse_root = lax.rsqrt(square)
        profile = jnp.exp(-(square * inverse_root))
        return profile, profile * inverse_root, along_x, along_y

    def lane_place(both, odd, at_y, groups, write):
        turn = jnp.bitwise_and(at_y, 127)
        block = jnp.right_shift(at_y - turn, 7)
        value = pltpu.roll(both, jnp.bitwise_and(turn + 128 - STAMP * odd, 127), 1)
        high, low = split(value)
        owner = jnp.where(lane16 >= turn, block, block + 1)
        owner = jnp.where(owner == -1, 2, owner)
        owner = jnp.where(jnp.bitwise_and(lane16 - turn, 127) < STAMP, owner, 3)
        for g in range(groups):
            keep = jnp.where(owner == g, 1.0, 0.0).astype(BF16)
            for r in range(0, STAMP, 16):
                write(g, 0, r, high[r : r + 16] * keep)
                write(g, 1, r, low[r : r + 16] * keep)

    keys, found = [], jnp.int32(0)
    edge_y = [jnp.int32(0)] * EDGES
    last = tile - STAMP
    for s in range(slots):
        at_x, at_y = offset_ref[0, 0, 0, s], offset_ref[1, 0, 0, s]
        reach = jnp.maximum(jnp.maximum(-at_x, at_x - last), jnp.maximum(-at_y, at_y - last))
        hit = jnp.where(s < live_count, reach, 0) > 0
        key = jnp.where(hit, found, -1)
        found = jnp.where(hit, found + 1, found)
        keys.append(key)
        edge_y = [jnp.where(key == k, at_y, edge_y[k]) for k in range(EDGES)]
    edge, edge_profiles = [], []
    for h in range(EDGES // 2):
        which = jnp.where(first_half, 2 * h, 2 * h + 1)
        values = [jnp.full((1, 128), v, F32) for v in (0.0, 0.0, 1.0, 0.0, 0.0, 0.0)]
        values.append(jnp.zeros((1, 128), jnp.int32))
        for s in range(slots):
            here = which == keys[s]
            new = [
                shift_ref[0, 0, 0, s],
                shift_ref[1, 0, 0, s],
                radius_ref[0, 0, s],
                ellipse_ref[0, 0, 0, s],
                ellipse_ref[1, 0, 0, s],
                flux_ref[0, 0, s],
                offset_ref[0, 0, 0, s],
            ]
            values = [jnp.where(here, n, v) for n, v in zip(new, values)]
        edge.append(values)
        edge_profiles.append(shape(*values[:5])[0])
    spread = blur_columns(jnp.concatenate(edge_profiles, axis=1))
    for k in range(EDGES):
        both = spread[:, 128 * (k // 2) : 128 * (k // 2 + 1)] * edge[k // 2][5]

        def write(g, part, r, value):
            start = 256 * part + 128 * g if g < 2 else 512 + 128 * part
            edge_lanes[STAMP * k + r : STAMP * k + r + 16, start : start + 128] = value

        lane_place(both, k % 2, edge_y[k], 3, write)
    edge_target = jnp.concatenate([values[6] + column1 for values in edge], axis=1)
    at = lax.broadcasted_iota(jnp.int32, (tile + 2 * MARGIN, STAMP * EDGES), 0)
    at = jnp.where(at < 2 * MARGIN, jnp.where(at < MARGIN, at - MARGIN, at - MARGIN + tile), at - 2 * MARGIN)
    place = jnp.where(at == edge_target, 1.0, 0.0).astype(BF16)
    high = jnp.dot(place, left_high, preferred_element_type=F32).astype(BF16)
    low = jnp.dot(place, left_low, preferred_element_type=F32).astype(BF16)
    first = 2 * MARGIN
    outer = jnp.dot(
        jnp.concatenate([high[:first], low[:first]], axis=0),
        edge_lanes[...],
        preferred_element_type=F32,
    )
    outer = outer[:first] + outer[first:]
    side = jnp.dot(
        jnp.concatenate([high[first:], low[first:]], axis=0),
        edge_lanes[:, 512:768],
        preferred_element_type=F32,
    )
    side = side[:tile] + side[tile:]
    side = side[:, 0:128] + side[:, 128:256]
    corners = outer[:, 512:640] + outer[:, 640:768]

    def pack(strip, first_lane):
        size = strip.shape[0] // 4
        place_in = lax.broadcasted_iota(jnp.int32, (size, 128), 1)
        out = None
        for c in range(4):
            turn = (32 * c + 128 - first_lane) % 128
            block = strip[size * c : size * (c + 1)]
            block = pltpu.roll(block, turn, 1) if turn else block
            out = block if c == 0 else jnp.where(place_in >= 32 * c, block, out)
        return out

    for p in range(2):
        strip = corners[MARGIN * p : MARGIN * (p + 1)]
        edge_rows[p] = outer[MARGIN * p : MARGIN * (p + 1), 0:256] + (
            outer[MARGIN * p : MARGIN * (p + 1), 256:512]
        )
        pack_sides[p] = pack(side, 96 - 96 * p)
        pack_corners[2 * p] = pack(strip, 96)
        pack_corners[2 * p + 1] = pack(strip, 0)

    sources = [pack_sides.at[d] for d in range(2)] + [pack_corners.at[d] for d in range(4)]
    sources += [edge_rows.at[d] for d in range(2)]
    landings = [in_sides.at[d] for d in range(2)] + [in_corners.at[d] for d in range(4)]
    landings += [in_rows.at[d] for d in range(2)]
    pl.semaphore_wait(barrier, len(peers) + sum(exists))
    halos = [
        pltpu.make_async_remote_copy(
            src_ref=sources[d],
            dst_ref=landings[d],
            send_sem=send_sems.at[d],
            recv_sem=recv_sems.at[d],
            device_id=around[d],
            device_id_type=MESH,
        )
        for d in range(8)
    ]
    for halo, there in zip(halos, exists):

        @pl.when(there == 1)
        def _():
            halo.start()

    for j in range(pairs):
        profile, scaled, along_x, along_y = shape(
            pair_of(j, shift_ref, 0, 0, 0),
            pair_of(j, shift_ref, 1, 0, 0),
            pair_of(j, radius_ref, 0, 0),
            pair_of(j, ellipse_ref, 0, 0, 0),
            pair_of(j, ellipse_ref, 1, 0, 0),
        )
        stack(stacked, profile, 128 * j)
        stack(stacked, scaled * along_x, STAMP * slots + 128 * j)
        stack(stacked, scaled * along_y, 2 * STAMP * slots + 128 * j)
    spread = blur(stacked, 3 * STAMP * slots)
    quads = slots // 4
    for k in range(3):
        for g in range(quads):
            start = STAMP * (quads * k + g)
            blurred[k, :, 256 * g : 256 * (g + 1)] = spread[start : start + STAMP]

    targets = []
    for j in range(pairs):
        slot = jnp.where(first_half, 2 * j, 2 * j + 1)
        flux = jnp.where(slot < live_count, pair_of(j, flux_ref, 0, 0), 0.0)
        both = blurred[0, :, 128 * j : 128 * (j + 1)] * flux
        for odd in range(2):
            s = 2 * j + odd

            def write(g, part, r, value):
                start = 256 * part + 128 * g
                lanes[STAMP * s + r : STAMP * s + r + 16, start : start + 128] = value

            lane_place(both, odd, offset_ref[1, 0, 0, s], 2, write)
        targets.append(pair_of(j, offset_ref, 0, 0, 0) + column1)
    target = jnp.concatenate(targets, axis=1)
    at = lax.broadcasted_iota(jnp.int32, (tile, slots * STAMP), 0)
    place = jnp.where(at == target, 1.0, 0.0).astype(BF16)
    placed = jnp.dot(place, lanes[...], preferred_element_type=F32)
    for fetch in fetches[len(small) :]:
        fetch.wait()
    remain_ref[0] = image[...] - (placed[:, :256] + placed[:, 256:])

    def fold(value):
        total = value[0:8]
        for r in range(8, STAMP, 8):
            total = total + value[r : r + 8]
        return total

    for j in range(pairs):
        at_x = row + pair_of(j, offset_ref, 0, 0, 0)
        at_y = column1 + pair_of(j, offset_ref, 1, 0, 0)
        inside = (at_x >= 0) & (at_x < tile) & (at_y >= 0) & (at_y < tile)
        own = slice(128 * j, 128 * (j + 1))
        masked = [jnp.where(inside, blurred[k, :, own], 0.0) for k in range(3)]
        for k in range(3):
            blurred[k, :, own] = masked[k]
        n = 0
        for k in range(3):
            for l in range(k, 3):
                partial[8 * n : 8 * (n + 1), own] = fold(masked[k] * masked[l])
                n += 1

    segment = jnp.where(
        jnp.right_shift(lax.broadcasted_iota(jnp.int32, (slots * STAMP, 128), 0), 6)
        == lax.broadcasted_iota(jnp.int32, (slots * STAMP, 128), 1),
        1.0,
        0.0,
    ).astype(BF16)

    def gather_sums(value):
        size = value.shape[0]
        out = jnp.dot(
            jnp.concatenate(split(value), axis=0), segment, preferred_element_type=F32
        )
        out = out[:size] + out[size:]
        return [
            jnp.sum(out[8 * k : 8 * (k + 1)], axis=0, keepdims=True) for k in range(size // 8)
        ]

    def shares_of(ref, send, recv):
        def share(slot, d):
            return pltpu.make_async_remote_copy(
                src_ref=ref.at[slot],
                dst_ref=ref.at[slot],
                send_sem=send.at[d - 1],
                recv_sem=recv.at[d - 1],
                device_id=peers[d - 1],
                device_id_type=MESH,
            )

        order = sorted(range(1, nb), key=lambda d: -min(d, nb - d))
        sent = [share(me, d) for d in order]
        for copy in sent:
            copy.start()
        return sent, [(share, lax.rem(me + nb - d, nb), d) for d in order]

    weight = weight_ref[0]
    normal = gather_sums(partial[0:48, :])
    normals[me] = weight * jnp.concatenate(normal + [jnp.zeros((2, 128), F32)], axis=0)
    sent, expected = shares_of(normals, normal_send, normal_recv)

    for r in range(MARGIN // 8):
        for g in range(2):
            blocks[r, g] = jnp.zeros((8, 128), F32)
            blocks[tile // 8 + MARGIN // 8 + r, g] = jnp.zeros((8, 128), F32)

    for d in range(8):

        @pl.when(exists[opposite[d]] == 1)
        def _():
            halos[d].wait_recv()

    ones = jnp.ones((1, 128), jnp.int32)
    has_up, has_down, has_left, has_right = [
        ones * there > 0 for there in (above, below, before, after)
    ]
    low_lanes = lane1 < MARGIN
    high_lanes = lane1 >= 128 - MARGIN

    def unpack(block, c, first_lane):
        turn = (first_lane + 128 - 32 * c) % 128
        return pltpu.roll(block, turn, 1) if turn else block

    def unpack_corner(block, first_lane):
        return jnp.concatenate([unpack(block, c, first_lane) for c in range(4)], axis=0)

    for c in range(4):
        for g in range(2):
            r0 = 64 * c
            own = slice(128 * g, 128 * (g + 1))
            if g == 0:
                total = jnp.where(low_lanes & has_left, unpack(in_sides[1], c, 0), 0.0)
            else:
                total = jnp.where(high_lanes & has_right, unpack(in_sides[0], c, 96), 0.0)
            if c == 0 or c == 3:
                there = has_up if c == 0 else has_down
                fringe = jnp.where(there, in_rows[1 if c == 0 else 0, :, own], 0.0)
                n = (3 if c == 0 else 1) - g
                corner = unpack_corner(in_corners[n], 96 * g)
                there = there & ((low_lanes & has_left) if g == 0 else (high_lanes & has_right))
                fringe = fringe + jnp.where(there, corner, 0.0)
                if c == 0:
                    total = jnp.concatenate([total[0:32] + fringe, total[32:64]], axis=0)
                else:
                    total = jnp.concatenate([total[0:32], total[32:64] + fringe], axis=0)
            value = remain_ref[0, r0 : r0 + 64, own] - total
            remain_ref[0, r0 : r0 + 64, own] = value
            for r in range(8):
                blocks[MARGIN // 8 + 8 * c + r, g] = value[8 * r : 8 * (r + 1)]

    sub = lax.broadcasted_iota(jnp.int32, (STAMP // 8, 8, 128), 1)
    for j in range(pairs):
        halves = []
        for odd in range(2):
            s = 2 * j + odd
            at_x = jnp.clip(offset_ref[0, 0, 0, s] + MARGIN, 0, tile - 1)
            step = jnp.bitwise_and(at_x, 7)
            first = jnp.right_shift(at_x, 3)
            at_y = offset_ref[1, 0, 0, s]
            turn = jnp.bitwise_and(at_y, 127)
            block = jnp.right_shift(at_y - turn, 7)
            take_one = jnp.where(lane1 >= turn, block, block + 1) >= 1
            value = jnp.stack(
                [
                    jnp.where(take_one, blocks[first + r, 1], blocks[first + r, 0])
                    for r in range(STAMP // 8 + 1)
                ]
            )
            value = pltpu.roll(value, jnp.bitwise_and(STAMP * odd + 256 - turn, 127), 2)
            value = pltpu.roll(value, jnp.bitwise_and(8 - step, 7), 1)
            value = jnp.where(sub < 8 - step, value[:-1], value[1:])
            halves.append(value.reshape(STAMP, 128))
        cutout = jnp.where(first_half, halves[0], halves[1])
        own = slice(128 * j, 128 * (j + 1))
        for k in range(3):
            partial[48 + 8 * k : 56 + 8 * k, own] = fold(blurred[k, :, own] * cutout)
    right = gather_sums(partial[48:72, :])
    right = right[0] + pltpu.roll(right[1], slots, 1) + pltpu.roll(right[2], 2 * slots, 1)
    rights[me] = weight * right
    more, others = shares_of(rights, right_send, right_recv)
    for share, slot, d in expected:
        share(slot, d).wait_recv()
    total = normals[0]
    for e in range(1, nb):
        total = total + normals[e]
    sums_ref[0:8] = total
    for share, slot, d in others:
        share(slot, d).wait_recv()
    total = rights[0]
    for e in range(1, nb):
        total = total + rights[e]
    sums_ref[8:9] = total
    sums_ref[9:10, 0:slots] = flux_vec[0]
    sums_ref[10:11, 0:slots] = shift_vec[0, 0]
    sums_ref[11:12, 0:slots] = shift_vec[1, 0]
    sums_ref[12:13, :] = jnp.where(lane1 < live_count, 1.0, 0.0)

    for share in sent + more:
        share.wait_send()
    for halo, there in zip(halos, exists):

        @pl.when(there == 1)
        def _():
            halo.wait_send()


def finish(sums_ref, remain_ref, refined_hbm, residual_hbm, refined, sems):
    store = pltpu.make_async_copy(remain_ref, residual_hbm, sems.at[0])
    store.start()
    slots = refined.shape[3]
    entry = [sums_ref[n : n + 1, 0:slots] for n in range(13)]
    start, live = entry[9], entry[12]
    flux = start * live
    m01, m02 = entry[1] * flux, entry[2] * flux
    m12 = entry[4] * flux * flux
    m00 = entry[0] + PRIOR
    m11 = entry[3] * flux * flux + PRIOR
    m22 = entry[5] * flux * flux + PRIOR
    right = [sums_ref[8:9, slots * k : slots * (k + 1)] for k in range(3)]
    v0, v1, v2 = right[0], right[1] * flux, right[2] * flux
    c00 = m11 * m22 - m12 * m12
    c01 = m12 * m02 - m01 * m22
    c02 = m01 * m12 - m11 * m02
    c11 = m00 * m22 - m02 * m02
    c12 = m01 * m02 - m00 * m12
    c22 = m00 * m11 - m01 * m01
    determinant = m00 * c00 + m01 * c01 + m02 * c02
    change = [
        (c00 * v0 + c01 * v1 + c02 * v2) / determinant,
        (c01 * v0 + c11 * v1 + c12 * v2) / determinant,
        (c02 * v0 + c12 * v1 + c22 * v2) / determinant,
    ]
    for k in range(3):
        refined[k, 0] = (entry[9 + k] + change[k]) * live
    write = pltpu.make_async_copy(refined, refined_hbm, sems.at[1])
    write.start()
    store.wait()
    write.wait()


def shards(
    image,
    psf_taps,
    exposure_weight,
    flux_start,
    centre_shift,
    radius,
    ellipticity,
    offsets,
    source_count,
):
    tile = image.shape[1]
    slots = flux_start.shape[2]
    rows = tile + 2 * MARGIN
    width = slots * STAMP
    vmem = pl.BlockSpec(memory_space=pltpu.VMEM)
    hbm = pl.BlockSpec(memory_space=pl.ANY)
    peers = lax.axis_size("be") - 1
    smem = pl.BlockSpec(memory_space=pltpu.SMEM)
    fetched = (psf_taps, flux_start, centre_shift, radius, ellipticity, offsets)
    sums, remain = pl.pallas_call(
        kernel,
        out_shape=(pltpu.VMEM((16, 128), F32), pltpu.VMEM(image.shape, F32)),
        in_specs=[hbm] * 2 + [smem] + [hbm] * 5 + [smem],
        out_specs=(vmem, vmem),
        scratch_shapes=[pltpu.SMEM(operand.shape, operand.dtype) for operand in fetched]
        + [
            pltpu.VMEM(flux_start.shape, F32),
            pltpu.VMEM(centre_shift.shape, F32),
            pltpu.VMEM((tile, tile), F32),
            pltpu.VMEM((EDGES * STAMP, 768), BF16),
            pltpu.VMEM((2, MARGIN, tile), F32),
            pltpu.VMEM((2, STAMP, 128), F32),
            pltpu.VMEM((4, 8, 128), F32),
            pltpu.VMEM((2, MARGIN, tile), F32),
            pltpu.VMEM((2, STAMP, 128), F32),
            pltpu.VMEM((4, 8, 128), F32),
            pltpu.VMEM((3 * STAMP, 3 * width), BF16),
            pltpu.VMEM((3, STAMP, width), F32),
            pltpu.VMEM((width, 2 * tile), BF16),
            pltpu.VMEM((rows // 8, 2, 8, 128), F32),
            pltpu.VMEM((72, width), F32),
            pltpu.VMEM((peers + 1, 8, 128), F32),
            pltpu.VMEM((peers + 1, 1, 128), F32),
            pltpu.SemaphoreType.DMA((9,)),
            pltpu.SemaphoreType.DMA((8,)),
            pltpu.SemaphoreType.DMA((8,)),
            pltpu.SemaphoreType.DMA((peers,)),
            pltpu.SemaphoreType.DMA((peers,)),
            pltpu.SemaphoreType.DMA((peers,)),
            pltpu.SemaphoreType.DMA((peers,)),
        ],
        compiler_params=pltpu.CompilerParams(collective_id=0, has_side_effects=True),
        name="photometry",
    )(
        image,
        psf_taps,
        exposure_weight,
        flux_start,
        centre_shift,
        radius,
        ellipticity,
        offsets,
        source_count,
    )
    sums = pltpu.with_memory_space_constraint(sums, pltpu.VMEM)
    remain = pltpu.with_memory_space_constraint(remain, pltpu.VMEM)
    return pl.pallas_call(
        finish,
        out_shape=(
            jax.ShapeDtypeStruct((3, 1, 1, slots), F32),
            jax.ShapeDtypeStruct(image.shape, F32),
        ),
        in_specs=[vmem, vmem],
        out_specs=(hbm, hbm),
        scratch_shapes=[pltpu.VMEM((3, 1, 1, slots), F32), pltpu.SemaphoreType.DMA((2,))],
        name="finish",
    )(sums, remain)


def solution(mesh):
    return jax.shard_map(
        shards,
        mesh=mesh,
        in_specs=(
            P("be", "skyx", "skyy"),
            P("be", None, None),
            P("be"),
            P("skyx", "skyy", None),
            P(None, "skyx", "skyy", None),
            P("skyx", "skyy", None),
            P(None, "skyx", "skyy", None),
            P(None, "skyx", "skyy", None),
            P("skyx", "skyy"),
        ),
        out_specs=(P(None, "skyx", "skyy", None), P("be", "skyx", "skyy")),
        check_vma=False,
    )
```

```python
import jax
import jax.numpy as jnp
from jax import lax
from jax.experimental import pallas as pl
from jax.experimental.pallas import tpu as pltpu
from jax.sharding import PartitionSpec as P

STAMP = 64
MARGIN = 32
TAPS = 15
PRIOR = 8.0
EDGES = 4
F32 = jnp.float32
BF16 = jnp.bfloat16
MESH = pl.DeviceIdType.MESH


def split(x):
    high = x.astype(BF16)
    return high, (x - high.astype(F32)).astype(BF16)


def band(taps_ref, which, differ):
    total = taps_ref[0, which, 0]
    for t in range(1, TAPS):
        total = total + taps_ref[0, which, t]
    out = jnp.zeros(differ.shape, F32)
    for t in range(TAPS):
        out = jnp.where(differ == t - TAPS // 2, taps_ref[0, which, t], out)
    return out / jnp.full(differ.shape, total, F32)


def kernel(
    image_hbm,
    taps_hbm,
    weight_ref,
    flux_hbm,
    shift_hbm,
    radius_hbm,
    ellipse_hbm,
    offset_hbm,
    count_ref,
    sums_ref,
    remain_ref,
    taps_ref,
    flux_ref,
    shift_ref,
    radius_ref,
    ellipse_ref,
    offset_ref,
    flux_vec,
    shift_vec,
    image,
    edge_lanes,
    edge_rows,
    pack_sides,
    pack_corners,
    in_rows,
    in_sides,
    in_corners,
    stacked,
    blurred,
    lanes,
    blocks,
    partial,
    normals,
    rights,
    copy_sems,
    send_sems,
    recv_sems,
    normal_send,
    normal_recv,
    right_send,
    right_recv,
):
    slots = flux_hbm.shape[2]
    tile = image_hbm.shape[1]
    pairs = slots // 2
    mx = lax.axis_index("skyx")
    my = lax.axis_index("skyy")
    me = lax.axis_index("be")
    nx = lax.axis_size("skyx")
    ny = lax.axis_size("skyy")
    nb = lax.axis_size("be")
    above, below = (mx > 0).astype(jnp.int32), (mx < nx - 1).astype(jnp.int32)
    before, after = (my > 0).astype(jnp.int32), (my < ny - 1).astype(jnp.int32)
    around = [
        (mx, my - before, me),
        (mx, my + after, me),
        (mx - above, my - before, me),
        (mx - above, my + after, me),
        (mx + below, my - before, me),
        (mx + below, my + after, me),
        (mx - above, my, me),
        (mx + below, my, me),
    ]
    exists = [
        before,
        after,
        above * before,
        above * after,
        below * before,
        below * after,
        above,
        below,
    ]
    opposite = [1, 0, 5, 4, 3, 2, 7, 6]
    peers = [(mx, my, lax.rem(me + d, nb)) for d in range(1, nb)]

    barrier = pltpu.get_barrier_semaphore()
    small = [
        (offset_hbm, offset_ref),
        (shift_hbm, shift_ref),
        (radius_hbm, radius_ref),
        (ellipse_hbm, ellipse_ref),
        (flux_hbm, flux_ref),
        (taps_hbm, taps_ref),
    ]
    late = [(image_hbm.at[0], image), (flux_hbm, flux_vec), (shift_hbm, shift_vec)]
    fetches = [
        pltpu.make_async_copy(source, target, copy_sems.at[n])
        for n, (source, target) in enumerate(small + late)
    ]
    for fetch in fetches[: len(small)]:
        fetch.start()
    for device, there in zip(around, exists):

        @pl.when(there == 1)
        def _():
            pl.semaphore_signal(barrier, inc=1, device_id=device, device_id_type=MESH)

    for device in peers:
        pl.semaphore_signal(barrier, inc=1, device_id=device, device_id_type=MESH)
    for fetch in fetches[len(small) :]:
        fetch.start()
    for fetch in fetches[: len(small)]:
        fetch.wait()

    row = lax.broadcasted_iota(jnp.int32, (STAMP, 128), 0)
    lane = lax.broadcasted_iota(jnp.int32, (STAMP, 128), 1)
    lane1 = lax.broadcasted_iota(jnp.int32, (1, 128), 1)
    lane16 = lax.broadcasted_iota(jnp.int32, (16, 128), 1)
    first_half = lane1 < STAMP
    column1 = jnp.where(first_half, lane1, lane1 - STAMP)
    grid_u = row.astype(F32)
    grid_v = column1.astype(F32)
    live_count = count_ref[0, 0]

    def pair_of(j, ref, *index):
        return jnp.where(first_half, ref[index + (2 * j,)], ref[index + (2 * j + 1,)])

    rows_band = jnp.where(lane < STAMP, band(taps_ref, 0, row - lane), 0.0)
    columns_band = jnp.where(lane < STAMP, band(taps_ref, 1, lane - row), 0.0)
    nothing = jnp.zeros((STAMP, 128), F32)

    def diagonal(block):
        other = pltpu.roll(block, STAMP, 1)
        return jnp.concatenate(
            [
                jnp.concatenate([block, nothing], axis=1),
                jnp.concatenate([other, nothing], axis=1),
                jnp.concatenate([nothing, block], axis=1),
                jnp.concatenate([nothing, other], axis=1),
            ],
            axis=0,
        )

    right_high, right_low = split(diagonal(columns_band))
    left_high, left_low = split(diagonal(rows_band))
    rows_high, rows_low = left_high[:STAMP, :STAMP], left_low[:STAMP, :STAMP]
    left_factor = jnp.concatenate([rows_high, rows_high, rows_low], axis=1)

    def blur_columns(groups):
        size = groups.shape[0]
        high, low = split(groups)
        out = jnp.dot(
            jnp.concatenate([high, low], axis=0), right_high, preferred_element_type=F32
        )
        return out[:size] + out[size:] + jnp.dot(high, right_low, preferred_element_type=F32)

    def blur(ref, width):
        along = jnp.dot(left_factor, ref[:, :width], preferred_element_type=F32)
        groups = jnp.concatenate(
            [along[:, 256 * g : 256 * (g + 1)] for g in range(width // 256)], axis=0
        )
        return blur_columns(groups)

    def stack(ref, value, start):
        high, low = split(value)
        ref[0:STAMP, start : start + 128] = high
        ref[STAMP : 2 * STAMP, start : start + 128] = low
        ref[2 * STAMP : 3 * STAMP, start : start + 128] = high

    def shape(shift_x, shift_y, radius, one, two):
        inverse = 1.0 / (radius * radius)
        coef_a = (1.0 + one) * inverse
        coef_b = two * inverse
        coef_c = (1.0 - one) * inverse
        u = grid_u - (float(STAMP // 2) + shift_x)
        v = grid_v - (float(STAMP // 2) + shift_y)
        along_x = coef_a * u + coef_b * v
        along_y = coef_b * u + coef_c * v
        square = u * along_x + v * along_y + 0.25
        inverse_root = lax.rsqrt(square)
        profile = jnp.exp(-(square * inverse_root))
        return profile, profile * inverse_root, along_x, along_y

    def lane_place(both, odd, at_y, groups, write):
        turn = jnp.bitwise_and(at_y, 127)
        block = jnp.right_shift(at_y - turn, 7)
        value = pltpu.roll(both, jnp.bitwise_and(turn + 128 - STAMP * odd, 127), 1)
        high, low = split(value)
        owner = jnp.where(lane16 >= turn, block, block + 1)
        owner = jnp.where(owner == -1, 2, owner)
        owner = jnp.where(jnp.bitwise_and(lane16 - turn, 127) < STAMP, owner, 3)
        for g in range(groups):
            keep = jnp.where(owner == g, 1.0, 0.0).astype(BF16)
            for r in range(0, STAMP, 16):
                write(g, 0, r, high[r : r + 16] * keep)
                write(g, 1, r, low[r : r + 16] * keep)

    keys, found = [], jnp.int32(0)
    edge_y = [jnp.int32(0)] * EDGES
    last = tile - STAMP
    for s in range(slots):
        at_x, at_y = offset_ref[0, 0, 0, s], offset_ref[1, 0, 0, s]
        reach = jnp.maximum(jnp.maximum(-at_x, at_x - last), jnp.maximum(-at_y, at_y - last))
        hit = jnp.where(s < live_count, reach, 0) > 0
        key = jnp.where(hit, found, -1)
        found = jnp.where(hit, found + 1, found)
        keys.append(key)
        edge_y = [jnp.where(key == k, at_y, edge_y[k]) for k in range(EDGES)]
    edge, edge_profiles = [], []
    for h in range(EDGES // 2):
        which = jnp.where(first_half, 2 * h, 2 * h + 1)
        values = [jnp.full((1, 128), v, F32) for v in (0.0, 0.0, 1.0, 0.0, 0.0, 0.0)]
        values.append(jnp.zeros((1, 128), jnp.int32))
        for s in range(slots):
            here = which == keys[s]
            new = [
                shift_ref[0, 0, 0, s],
                shift_ref[1, 0, 0, s],
                radius_ref[0, 0, s],
                ellipse_ref[0, 0, 0, s],
                ellipse_ref[1, 0, 0, s],
                flux_ref[0, 0, s],
                offset_ref[0, 0, 0, s],
            ]
            values = [jnp.where(here, n, v) for n, v in zip(new, values)]
        edge.append(values)
        edge_profiles.append(shape(*values[:5])[0])
    spread = blur_columns(jnp.concatenate(edge_profiles, axis=1))
    for k in range(EDGES):
        both = spread[:, 128 * (k // 2) : 128 * (k // 2 + 1)] * edge[k // 2][5]

        def write(g, part, r, value):
            start = 256 * part + 128 * g if g < 2 else 512 + 128 * part
            edge_lanes[STAMP * k + r : STAMP * k + r + 16, start : start + 128] = value

        lane_place(both, k % 2, edge_y[k], 3, write)
    edge_target = jnp.concatenate([values[6] + column1 for values in edge], axis=1)
    at = lax.broadcasted_iota(jnp.int32, (tile + 2 * MARGIN, STAMP * EDGES), 0)
    at = jnp.where(at < 2 * MARGIN, jnp.where(at < MARGIN, at - MARGIN, at - MARGIN + tile), at - 2 * MARGIN)
    place = jnp.where(at == edge_target, 1.0, 0.0).astype(BF16)
    high = jnp.dot(place, left_high, preferred_element_type=F32).astype(BF16)
    low = jnp.dot(place, left_low, preferred_element_type=F32).astype(BF16)
    first = 2 * MARGIN
    outer = jnp.dot(
        jnp.concatenate([high[:first], low[:first]], axis=0),
        edge_lanes[...],
        preferred_element_type=F32,
    )
    outer = outer[:first] + outer[first:]
    side = jnp.dot(
        jnp.concatenate([high[first:], low[first:]], axis=0),
        edge_lanes[:, 512:768],
        preferred_element_type=F32,
    )
    side = side[:tile] + side[tile:]
    side = side[:, 0:128] + side[:, 128:256]
    corners = outer[:, 512:640] + outer[:, 640:768]

    def pack(strip, first_lane):
        size = strip.shape[0] // 4
        place_in = lax.broadcasted_iota(jnp.int32, (size, 128), 1)
        out = None
        for c in range(4):
            turn = (32 * c + 128 - first_lane) % 128
            block = strip[size * c : size * (c + 1)]
            block = pltpu.roll(block, turn, 1) if turn else block
            out = block if c == 0 else jnp.where(place_in >= 32 * c, block, out)
        return out

    for p in range(2):
        strip = corners[MARGIN * p : MARGIN * (p + 1)]
        edge_rows[p] = outer[MARGIN * p : MARGIN * (p + 1), 0:256] + (
            outer[MARGIN * p : MARGIN * (p + 1), 256:512]
        )
        pack_sides[p] = pack(side, 96 - 96 * p)
        pack_corners[2 * p] = pack(strip, 96)
        pack_corners[2 * p + 1] = pack(strip, 0)

    sources = [pack_sides.at[d] for d in range(2)] + [pack_corners.at[d] for d in range(4)]
    sources += [edge_rows.at[d] for d in range(2)]
    landings = [in_sides.at[d] for d in range(2)] + [in_corners.at[d] for d in range(4)]
    landings += [in_rows.at[d] for d in range(2)]
    pl.semaphore_wait(barrier, len(peers) + sum(exists))
    halos = [
        pltpu.make_async_remote_copy(
            src_ref=sources[d],
            dst_ref=landings[d],
            send_sem=send_sems.at[d],
            recv_sem=recv_sems.at[d],
            device_id=around[d],
            device_id_type=MESH,
        )
        for d in range(8)
    ]
    for halo, there in zip(halos, exists):

        @pl.when(there == 1)
        def _():
            halo.start()

    for j in range(pairs):
        profile, scaled, along_x, along_y = shape(
            pair_of(j, shift_ref, 0, 0, 0),
            pair_of(j, shift_ref, 1, 0, 0),
            pair_of(j, radius_ref, 0, 0),
            pair_of(j, ellipse_ref, 0, 0, 0),
            pair_of(j, ellipse_ref, 1, 0, 0),
        )
        stack(stacked, profile, 128 * j)
        stack(stacked, scaled * along_x, STAMP * slots + 128 * j)
        stack(stacked, scaled * along_y, 2 * STAMP * slots + 128 * j)
    spread = blur(stacked, 3 * STAMP * slots)
    quads = slots // 4
    for k in range(3):
        for g in range(quads):
            start = STAMP * (quads * k + g)
            blurred[k, :, 256 * g : 256 * (g + 1)] = spread[start : start + STAMP]

    targets = []
    for j in range(pairs):
        slot = jnp.where(first_half, 2 * j, 2 * j + 1)
        flux = jnp.where(slot < live_count, pair_of(j, flux_ref, 0, 0), 0.0)
        both = blurred[0, :, 128 * j : 128 * (j + 1)] * flux
        for odd in range(2):
            s = 2 * j + odd

            def write(g, part, r, value):
                start = 256 * part + 128 * g
                lanes[STAMP * s + r : STAMP * s + r + 16, start : start + 128] = value

            lane_place(both, odd, offset_ref[1, 0, 0, s], 2, write)
        targets.append(pair_of(j, offset_ref, 0, 0, 0) + column1)
    target = jnp.concatenate(targets, axis=1)
    at = lax.broadcasted_iota(jnp.int32, (tile, slots * STAMP), 0)
    place = jnp.where(at == target, 1.0, 0.0).astype(BF16)
    placed = jnp.dot(place, lanes[...], preferred_element_type=F32)
    for fetch in fetches[len(small) :]:
        fetch.wait()
    remain_ref[0] = image[...] - (placed[:, :256] + placed[:, 256:])

    def fold(value):
        total = value[0:8]
        for r in range(8, STAMP, 8):
            total = total + value[r : r + 8]
        return total

    for j in range(pairs):
        at_x = row + pair_of(j, offset_ref, 0, 0, 0)
        at_y = column1 + pair_of(j, offset_ref, 1, 0, 0)
        inside = (at_x >= 0) & (at_x < tile) & (at_y >= 0) & (at_y < tile)
        own = slice(128 * j, 128 * (j + 1))
        masked = [jnp.where(inside, blurred[k, :, own], 0.0) for k in range(3)]
        for k in range(3):
            blurred[k, :, own] = masked[k]
        n = 0
        for k in range(3):
            for l in range(k, 3):
                partial[8 * n : 8 * (n + 1), own] = fold(masked[k] * masked[l])
                n += 1

    segment = jnp.where(
        jnp.right_shift(lax.broadcasted_iota(jnp.int32, (slots * STAMP, 128), 0), 6)
        == lax.broadcasted_iota(jnp.int32, (slots * STAMP, 128), 1),
        1.0,
        0.0,
    ).astype(BF16)

    def gather_sums(value):
        size = value.shape[0]
        out = jnp.dot(
            jnp.concatenate(split(value), axis=0), segment, preferred_element_type=F32
        )
        out = out[:size] + out[size:]
        return [
            jnp.sum(out[8 * k : 8 * (k + 1)], axis=0, keepdims=True) for k in range(size // 8)
        ]

    def shares_of(ref, send, recv):
        def share(slot, d):
            return pltpu.make_async_remote_copy(
                src_ref=ref.at[slot],
                dst_ref=ref.at[slot],
                send_sem=send.at[d - 1],
                recv_sem=recv.at[d - 1],
                device_id=peers[d - 1],
                device_id_type=MESH,
            )

        order = sorted(range(1, nb), key=lambda d: -min(d, nb - d))
        sent = [share(me, d) for d in order]
        for copy in sent:
            copy.start()
        return sent, [(share, lax.rem(me + nb - d, nb), d) for d in order]

    weight = weight_ref[0]
    normal = gather_sums(partial[0:48, :])
    normals[me] = weight * jnp.concatenate(normal + [jnp.zeros((2, 128), F32)], axis=0)
    sent, expected = shares_of(normals, normal_send, normal_recv)

    for r in range(MARGIN // 8):
        for g in range(2):
            blocks[r, g] = jnp.zeros((8, 128), F32)
            blocks[tile // 8 + MARGIN // 8 + r, g] = jnp.zeros((8, 128), F32)

    for d in range(8):

        @pl.when(exists[opposite[d]] == 1)
        def _():
            halos[d].wait_recv()

    ones = jnp.ones((1, 128), jnp.int32)
    has_up, has_down, has_left, has_right = [
        ones * there > 0 for there in (above, below, before, after)
    ]
    low_lanes = lane1 < MARGIN
    high_lanes = lane1 >= 128 - MARGIN

    def unpack(block, c, first_lane):
        turn = (first_lane + 128 - 32 * c) % 128
        return pltpu.roll(block, turn, 1) if turn else block

    def unpack_corner(block, first_lane):
        return jnp.concatenate([unpack(block, c, first_lane) for c in range(4)], axis=0)

    for c in range(4):
        for g in range(2):
            r0 = 64 * c
            own = slice(128 * g, 128 * (g + 1))
            if g == 0:
                total = jnp.where(low_lanes & has_left, unpack(in_sides[1], c, 0), 0.0)
            else:
                total = jnp.where(high_lanes & has_right, unpack(in_sides[0], c, 96), 0.0)
            if c == 0 or c == 3:
                there = has_up if c == 0 else has_down
                fringe = jnp.where(there, in_rows[1 if c == 0 else 0, :, own], 0.0)
                n = (3 if c == 0 else 1) - g
                corner = unpack_corner(in_corners[n], 96 * g)
                there = there & ((low_lanes & has_left) if g == 0 else (high_lanes & has_right))
                fringe = fringe + jnp.where(there, corner, 0.0)
                if c == 0:
                    total = jnp.concatenate([total[0:32] + fringe, total[32:64]], axis=0)
                else:
                    total = jnp.concatenate([total[0:32], total[32:64] + fringe], axis=0)
            value = remain_ref[0, r0 : r0 + 64, own] - total
            remain_ref[0, r0 : r0 + 64, own] = value
            for r in range(8):
                blocks[MARGIN // 8 + 8 * c + r, g] = value[8 * r : 8 * (r + 1)]

    sub = lax.broadcasted_iota(jnp.int32, (STAMP // 8, 8, 128), 1)
    for j in range(pairs):
        halves = []
        for odd in range(2):
            s = 2 * j + odd
            at_x = jnp.clip(offset_ref[0, 0, 0, s] + MARGIN, 0, tile - 1)
            step = jnp.bitwise_and(at_x, 7)
            first = jnp.right_shift(at_x, 3)
            at_y = offset_ref[1, 0, 0, s]
            turn = jnp.bitwise_and(at_y, 127)
            block = jnp.right_shift(at_y - turn, 7)
            take_one = jnp.where(lane1 >= turn, block, block + 1) >= 1
            value = jnp.stack(
                [
                    jnp.where(take_one, blocks[first + r, 1], blocks[first + r, 0])
                    for r in range(STAMP // 8 + 1)
                ]
            )
            value = pltpu.roll(value, jnp.bitwise_and(STAMP * odd + 256 - turn, 127), 2)
            value = pltpu.roll(value, jnp.bitwise_and(8 - step, 7), 1)
            value = jnp.where(sub < 8 - step, value[:-1], value[1:])
            halves.append(value.reshape(STAMP, 128))
        cutout = jnp.where(first_half, halves[0], halves[1])
        own = slice(128 * j, 128 * (j + 1))
        for k in range(3):
            partial[48 + 8 * k : 56 + 8 * k, own] = fold(blurred[k, :, own] * cutout)
    right = gather_sums(partial[48:72, :])
    right = right[0] + pltpu.roll(right[1], slots, 1) + pltpu.roll(right[2], 2 * slots, 1)
    rights[me] = weight * right
    more, others = shares_of(rights, right_send, right_recv)

    for halo, there in zip(halos, exists):

        @pl.when(there == 1)
        def _():
            halo.wait_send()

    for share in sent:
        share.wait_send()
    for share, slot, d in expected:
        share(slot, d).wait_recv()
    total = normals[0]
    for e in range(1, nb):
        total = total + normals[e]
    entry = [total[n : n + 1, 0:slots] for n in range(6)]
    live = lax.broadcasted_iota(jnp.int32, (1, slots), 1) < live_count
    flux = jnp.where(live, flux_vec[0], 0.0)
    m00, m01, m02 = entry[0] + PRIOR, entry[1] * flux, entry[2] * flux
    m11, m12 = entry[3] * flux * flux + PRIOR, entry[4] * flux * flux
    m22 = entry[5] * flux * flux + PRIOR
    c00 = m11 * m22 - m12 * m12
    c01 = m12 * m02 - m01 * m22
    c02 = m01 * m12 - m11 * m02
    c11 = m00 * m22 - m02 * m02
    c12 = m01 * m02 - m00 * m12
    c22 = m00 * m11 - m01 * m01
    scale = jnp.where(live, 1.0, 0.0) / (m00 * c00 + m01 * c01 + m02 * c02)
    rows = [c00, c01, c02, c01, c11, c12, c02, c12, c22]
    for n in range(9):
        sums_ref[n : n + 1, 0:slots] = rows[n] * (scale if n % 3 == 0 else scale * flux)
    bases = [flux_vec[0], shift_vec[0, 0], shift_vec[1, 0]]
    for k in range(3):
        sums_ref[9 + k : 10 + k, 0:slots] = jnp.where(live, bases[k], 0.0)

    for share, slot, d in others:
        share(slot, d).wait_recv()
    total = rights[0]
    for e in range(1, nb):
        total = total + rights[e]
    sums_ref[12:13] = total
    for share in more:
        share.wait_send()


def finish(sums_ref, remain_ref, refined_hbm, residual_hbm, refined, sems):
    store = pltpu.make_async_copy(remain_ref, residual_hbm, sems.at[0])
    store.start()
    slots = refined.shape[3]
    right = [sums_ref[12:13, slots * k : slots * (k + 1)] for k in range(3)]
    for k in range(3):
        value = sums_ref[9 + k : 10 + k, 0:slots]
        for l in range(3):
            value = value + sums_ref[3 * k + l : 3 * k + l + 1, 0:slots] * right[l]
        refined[k, 0] = value
    write = pltpu.make_async_copy(refined, refined_hbm, sems.at[1])
    write.start()
    store.wait()
    write.wait()


def shards(
    image,
    psf_taps,
    exposure_weight,
    flux_start,
    centre_shift,
    radius,
    ellipticity,
    offsets,
    source_count,
):
    tile = image.shape[1]
    slots = flux_start.shape[2]
    rows = tile + 2 * MARGIN
    width = slots * STAMP
    vmem = pl.BlockSpec(memory_space=pltpu.VMEM)
    hbm = pl.BlockSpec(memory_space=pl.ANY)
    peers = lax.axis_size("be") - 1
    smem = pl.BlockSpec(memory_space=pltpu.SMEM)
    fetched = (psf_taps, flux_start, centre_shift, radius, ellipticity, offsets)
    sums, remain = pl.pallas_call(
        kernel,
        out_shape=(pltpu.VMEM((16, 128), F32), pltpu.VMEM(image.shape, F32)),
        in_specs=[hbm] * 2 + [smem] + [hbm] * 5 + [smem],
        out_specs=(vmem, vmem),
        scratch_shapes=[pltpu.SMEM(operand.shape, operand.dtype) for operand in fetched]
        + [
            pltpu.VMEM(flux_start.shape, F32),
            pltpu.VMEM(centre_shift.shape, F32),
            pltpu.VMEM((tile, tile), F32),
            pltpu.VMEM((EDGES * STAMP, 768), BF16),
            pltpu.VMEM((2, MARGIN, tile), F32),
            pltpu.VMEM((2, STAMP, 128), F32),
            pltpu.VMEM((4, 8, 128), F32),
            pltpu.VMEM((2, MARGIN, tile), F32),
            pltpu.VMEM((2, STAMP, 128), F32),
            pltpu.VMEM((4, 8, 128), F32),
            pltpu.VMEM((3 * STAMP, 3 * width), BF16),
            pltpu.VMEM((3, STAMP, width), F32),
            pltpu.VMEM((width, 2 * tile), BF16),
            pltpu.VMEM((rows // 8, 2, 8, 128), F32),
            pltpu.VMEM((72, width), F32),
            pltpu.VMEM((peers + 1, 8, 128), F32),
            pltpu.VMEM((peers + 1, 1, 128), F32),
            pltpu.SemaphoreType.DMA((9,)),
            pltpu.SemaphoreType.DMA((8,)),
            pltpu.SemaphoreType.DMA((8,)),
            pltpu.SemaphoreType.DMA((peers,)),
            pltpu.SemaphoreType.DMA((peers,)),
            pltpu.SemaphoreType.DMA((peers,)),
            pltpu.SemaphoreType.DMA((peers,)),
        ],
        compiler_params=pltpu.CompilerParams(collective_id=0, has_side_effects=True),
        name="photometry",
    )(
        image,
        psf_taps,
        exposure_weight,
        flux_start,
        centre_shift,
        radius,
        ellipticity,
        offsets,
        source_count,
    )
    sums = pltpu.with_memory_space_constraint(sums, pltpu.VMEM)
    remain = pltpu.with_memory_space_constraint(remain, pltpu.VMEM)
    return pl.pallas_call(
        finish,
        out_shape=(
            jax.ShapeDtypeStruct((3, 1, 1, slots), F32),
            jax.ShapeDtypeStruct(image.shape, F32),
        ),
        in_specs=[vmem, vmem],
        out_specs=(hbm, hbm),
        scratch_shapes=[pltpu.VMEM((3, 1, 1, slots), F32), pltpu.SemaphoreType.DMA((2,))],
        name="finish",
    )(sums, remain)


def solution(mesh):
    return jax.shard_map(
        shards,
        mesh=mesh,
        in_specs=(
            P("be", "skyx", "skyy"),
            P("be", None, None),
            P("be"),
            P("skyx", "skyy", None),
            P(None, "skyx", "skyy", None),
            P("skyx", "skyy", None),
            P(None, "skyx", "skyy", None),
            P(None, "skyx", "skyy", None),
            P("skyx", "skyy"),
        ),
        out_specs=(P(None, "skyx", "skyy", None), P("be", "skyx", "skyy")),
        check_vma=False,
    )
```

```python
import jax
import jax.numpy as jnp
from jax import lax
from jax.experimental import pallas as pl
from jax.experimental.pallas import tpu as pltpu
from jax.sharding import PartitionSpec as P

STAMP = 64
MARGIN = 32
TAPS = 15
PRIOR = 8.0
EDGES = 4
F32 = jnp.float32
BF16 = jnp.bfloat16
MESH = pl.DeviceIdType.MESH


def split(x):
    high = x.astype(BF16)
    return high, (x - high.astype(F32)).astype(BF16)


def band(taps_ref, which, differ):
    total = taps_ref[0, which, 0]
    for t in range(1, TAPS):
        total = total + taps_ref[0, which, t]
    out = jnp.zeros(differ.shape, F32)
    for t in range(TAPS):
        out = jnp.where(differ == t - TAPS // 2, taps_ref[0, which, t], out)
    return out / jnp.full(differ.shape, total, F32)


def kernel(
    image_hbm,
    taps_hbm,
    weight_ref,
    flux_hbm,
    shift_hbm,
    radius_hbm,
    ellipse_hbm,
    offset_hbm,
    count_ref,
    sums_ref,
    remain_ref,
    taps_ref,
    flux_ref,
    shift_ref,
    radius_ref,
    ellipse_ref,
    offset_ref,
    flux_vec,
    shift_vec,
    image,
    edge_lanes,
    edge_rows,
    pack_sides,
    pack_corners,
    in_rows,
    in_sides,
    in_corners,
    stacked,
    blurred,
    lanes,
    blocks,
    shifted,
    partial,
    normals,
    rights,
    copy_sems,
    send_sems,
    recv_sems,
    normal_send,
    normal_recv,
    right_send,
    right_recv,
):
    slots = flux_hbm.shape[2]
    tile = image_hbm.shape[1]
    pairs = slots // 2
    mx = lax.axis_index("skyx")
    my = lax.axis_index("skyy")
    me = lax.axis_index("be")
    nx = lax.axis_size("skyx")
    ny = lax.axis_size("skyy")
    nb = lax.axis_size("be")
    above, below = (mx > 0).astype(jnp.int32), (mx < nx - 1).astype(jnp.int32)
    before, after = (my > 0).astype(jnp.int32), (my < ny - 1).astype(jnp.int32)
    around = [
        (mx, my - before, me),
        (mx, my + after, me),
        (mx - above, my - before, me),
        (mx - above, my + after, me),
        (mx + below, my - before, me),
        (mx + below, my + after, me),
        (mx - above, my, me),
        (mx + below, my, me),
    ]
    exists = [
        before,
        after,
        above * before,
        above * after,
        below * before,
        below * after,
        above,
        below,
    ]
    opposite = [1, 0, 5, 4, 3, 2, 7, 6]
    peers = [(mx, my, lax.rem(me + d, nb)) for d in range(1, nb)]

    barrier = pltpu.get_barrier_semaphore()
    for device, there in zip(around, exists):

        @pl.when(there == 1)
        def _():
            pl.semaphore_signal(barrier, inc=1, device_id=device, device_id_type=MESH)

    small = [
        (offset_hbm, offset_ref),
        (shift_hbm, shift_ref),
        (radius_hbm, radius_ref),
        (ellipse_hbm, ellipse_ref),
        (flux_hbm, flux_ref),
        (taps_hbm, taps_ref),
    ]
    late = [(image_hbm.at[0], image), (flux_hbm, flux_vec), (shift_hbm, shift_vec)]
    fetches = [
        pltpu.make_async_copy(source, target, copy_sems.at[n])
        for n, (source, target) in enumerate(small + late)
    ]
    for fetch in fetches[: len(small)]:
        fetch.start()
    for device in peers:
        pl.semaphore_signal(barrier, inc=1, device_id=device, device_id_type=MESH)
    for fetch in fetches[len(small) :]:
        fetch.start()
    for fetch in fetches[: len(small)]:
        fetch.wait()

    row = lax.broadcasted_iota(jnp.int32, (STAMP, 128), 0)
    lane = lax.broadcasted_iota(jnp.int32, (STAMP, 128), 1)
    lane1 = lax.broadcasted_iota(jnp.int32, (1, 128), 1)
    lane16 = lax.broadcasted_iota(jnp.int32, (16, 128), 1)
    first_half = lane1 < STAMP
    column1 = jnp.where(first_half, lane1, lane1 - STAMP)
    grid_u = row.astype(F32)
    grid_v = column1.astype(F32)
    live_count = count_ref[0, 0]

    def pair_of(j, ref, *index):
        return jnp.where(first_half, ref[index + (2 * j,)], ref[index + (2 * j + 1,)])

    rows_band = jnp.where(lane < STAMP, band(taps_ref, 0, row - lane), 0.0)
    columns_band = jnp.where(lane < STAMP, band(taps_ref, 1, lane - row), 0.0)
    nothing = jnp.zeros((STAMP, 128), F32)

    def diagonal(block):
        other = pltpu.roll(block, STAMP, 1)
        return jnp.concatenate(
            [
                jnp.concatenate([block, nothing], axis=1),
                jnp.concatenate([other, nothing], axis=1),
                jnp.concatenate([nothing, block], axis=1),
                jnp.concatenate([nothing, other], axis=1),
            ],
            axis=0,
        )

    right_high, right_low = split(diagonal(columns_band))
    left_high, left_low = split(diagonal(rows_band))
    rows_high, rows_low = left_high[:STAMP, :STAMP], left_low[:STAMP, :STAMP]
    left_factor = jnp.concatenate([rows_high, rows_high, rows_low], axis=1)

    def blur_columns(groups):
        size = groups.shape[0]
        high, low = split(groups)
        out = jnp.dot(
            jnp.concatenate([high, low], axis=0), right_high, preferred_element_type=F32
        )
        return out[:size] + out[size:] + jnp.dot(high, right_low, preferred_element_type=F32)

    def blur(ref, width):
        along = jnp.dot(left_factor, ref[:, :width], preferred_element_type=F32)
        groups = jnp.concatenate(
            [along[:, 256 * g : 256 * (g + 1)] for g in range(width // 256)], axis=0
        )
        return blur_columns(groups)

    def stack(ref, value, start):
        high, low = split(value)
        ref[0:STAMP, start : start + 128] = high
        ref[STAMP : 2 * STAMP, start : start + 128] = low
        ref[2 * STAMP : 3 * STAMP, start : start + 128] = high

    def shape(shift_x, shift_y, radius, one, two):
        inverse = 1.0 / (radius * radius)
        coef_a = (1.0 + one) * inverse
        coef_b = two * inverse
        coef_c = (1.0 - one) * inverse
        u = grid_u - (float(STAMP // 2) + shift_x)
        v = grid_v - (float(STAMP // 2) + shift_y)
        along_x = coef_a * u + coef_b * v
        along_y = coef_b * u + coef_c * v
        square = u * along_x + v * along_y + 0.25
        inverse_root = lax.rsqrt(square)
        profile = jnp.exp(-(square * inverse_root))
        return profile, profile * inverse_root, along_x, along_y

    def lane_place(both, odd, at_y, groups, write):
        turn = jnp.bitwise_and(at_y, 127)
        block = jnp.right_shift(at_y - turn, 7)
        value = pltpu.roll(both, jnp.bitwise_and(turn + 128 - STAMP * odd, 127), 1)
        high, low = split(value)
        owner = jnp.where(lane16 >= turn, block, block + 1)
        owner = jnp.where(owner == -1, 2, owner)
        owner = jnp.where(jnp.bitwise_and(lane16 - turn, 127) < STAMP, owner, 3)
        for g in range(groups):
            keep = jnp.where(owner == g, 1.0, 0.0).astype(BF16)
            for r in range(0, STAMP, 16):
                write(g, 0, r, high[r : r + 16] * keep)
                write(g, 1, r, low[r : r + 16] * keep)

    keys, found = [], jnp.int32(0)
    edge_y = [jnp.int32(0)] * EDGES
    last = tile - STAMP
    for s in range(slots):
        at_x, at_y = offset_ref[0, 0, 0, s], offset_ref[1, 0, 0, s]
        reach = jnp.maximum(jnp.maximum(-at_x, at_x - last), jnp.maximum(-at_y, at_y - last))
        hit = jnp.where(s < live_count, reach, 0) > 0
        key = jnp.where(hit, found, -1)
        found = jnp.where(hit, found + 1, found)
        keys.append(key)
        edge_y = [jnp.where(key == k, at_y, edge_y[k]) for k in range(EDGES)]
    edge, edge_profiles = [], []
    for h in range(EDGES // 2):
        which = jnp.where(first_half, 2 * h, 2 * h + 1)
        values = [jnp.full((1, 128), v, F32) for v in (0.0, 0.0, 1.0, 0.0, 0.0, 0.0)]
        values.append(jnp.zeros((1, 128), jnp.int32))
        for s in range(slots):
            here = which == keys[s]
            new = [
                shift_ref[0, 0, 0, s],
                shift_ref[1, 0, 0, s],
                radius_ref[0, 0, s],
                ellipse_ref[0, 0, 0, s],
                ellipse_ref[1, 0, 0, s],
                flux_ref[0, 0, s],
                offset_ref[0, 0, 0, s],
            ]
            values = [jnp.where(here, n, v) for n, v in zip(new, values)]
        edge.append(values)
        edge_profiles.append(shape(*values[:5])[0])
    spread = blur_columns(jnp.concatenate(edge_profiles, axis=1))
    for k in range(EDGES):
        both = spread[:, 128 * (k // 2) : 128 * (k // 2 + 1)] * edge[k // 2][5]

        def write(g, part, r, value):
            start = 256 * part + 128 * g if g < 2 else 512 + 128 * part
            edge_lanes[STAMP * k + r : STAMP * k + r + 16, start : start + 128] = value

        lane_place(both, k % 2, edge_y[k], 3, write)
    edge_target = jnp.concatenate([values[6] + column1 for values in edge], axis=1)
    at = lax.broadcasted_iota(jnp.int32, (tile + 2 * MARGIN, STAMP * EDGES), 0)
    at = jnp.where(at < 2 * MARGIN, jnp.where(at < MARGIN, at - MARGIN, at - MARGIN + tile), at - 2 * MARGIN)
    place = jnp.where(at == edge_target, 1.0, 0.0).astype(BF16)
    high = jnp.dot(place, left_high, preferred_element_type=F32).astype(BF16)
    low = jnp.dot(place, left_low, preferred_element_type=F32).astype(BF16)
    first = 2 * MARGIN
    outer = jnp.dot(
        jnp.concatenate([high[:first], low[:first]], axis=0),
        edge_lanes[...],
        preferred_element_type=F32,
    )
    outer = outer[:first] + outer[first:]
    side = jnp.dot(
        jnp.concatenate([high[first:], low[first:]], axis=0),
        edge_lanes[:, 512:768],
        preferred_element_type=F32,
    )
    side = side[:tile] + side[tile:]
    side = side[:, 0:128] + side[:, 128:256]
    corners = outer[:, 512:640] + outer[:, 640:768]

    def pack(strip, first_lane):
        size = strip.shape[0] // 4
        place_in = lax.broadcasted_iota(jnp.int32, (size, 128), 1)
        out = None
        for c in range(4):
            turn = (32 * c + 128 - first_lane) % 128
            block = strip[size * c : size * (c + 1)]
            block = pltpu.roll(block, turn, 1) if turn else block
            out = block if c == 0 else jnp.where(place_in >= 32 * c, block, out)
        return out

    for p in range(2):
        strip = corners[MARGIN * p : MARGIN * (p + 1)]
        edge_rows[p] = outer[MARGIN * p : MARGIN * (p + 1), 0:256] + (
            outer[MARGIN * p : MARGIN * (p + 1), 256:512]
        )
        pack_sides[p] = pack(side, 96 - 96 * p)
        pack_corners[2 * p] = pack(strip, 96)
        pack_corners[2 * p + 1] = pack(strip, 0)

    sources = [pack_sides.at[d] for d in range(2)] + [pack_corners.at[d] for d in range(4)]
    sources += [edge_rows.at[d] for d in range(2)]
    landings = [in_sides.at[d] for d in range(2)] + [in_corners.at[d] for d in range(4)]
    landings += [in_rows.at[d] for d in range(2)]
    pl.semaphore_wait(barrier, len(peers) + sum(exists))
    halos = [
        pltpu.make_async_remote_copy(
            src_ref=sources[d],
            dst_ref=landings[d],
            send_sem=send_sems.at[d],
            recv_sem=recv_sems.at[d],
            device_id=around[d],
            device_id_type=MESH,
        )
        for d in range(8)
    ]
    for halo, there in zip(halos, exists):

        @pl.when(there == 1)
        def _():
            halo.start()

    for j in range(pairs):
        profile, scaled, along_x, along_y = shape(
            pair_of(j, shift_ref, 0, 0, 0),
            pair_of(j, shift_ref, 1, 0, 0),
            pair_of(j, radius_ref, 0, 0),
            pair_of(j, ellipse_ref, 0, 0, 0),
            pair_of(j, ellipse_ref, 1, 0, 0),
        )
        stack(stacked, profile, 128 * j)
        stack(stacked, scaled * along_x, STAMP * slots + 128 * j)
        stack(stacked, scaled * along_y, 2 * STAMP * slots + 128 * j)
    spread = blur(stacked, 3 * STAMP * slots)
    quads = slots // 4
    for k in range(3):
        for g in range(quads):
            start = STAMP * (quads * k + g)
            blurred[k, :, 256 * g : 256 * (g + 1)] = spread[start : start + STAMP]

    targets = []
    for j in range(pairs):
        slot = jnp.where(first_half, 2 * j, 2 * j + 1)
        flux = jnp.where(slot < live_count, pair_of(j, flux_ref, 0, 0), 0.0)
        both = blurred[0, :, 128 * j : 128 * (j + 1)] * flux
        for odd in range(2):
            s = 2 * j + odd

            def write(g, part, r, value):
                start = 256 * part + 128 * g
                lanes[STAMP * s + r : STAMP * s + r + 16, start : start + 128] = value

            lane_place(both, odd, offset_ref[1, 0, 0, s], 2, write)
        targets.append(pair_of(j, offset_ref, 0, 0, 0) + column1)
    target = jnp.concatenate(targets, axis=1)
    at = lax.broadcasted_iota(jnp.int32, (tile, slots * STAMP), 0)
    place = jnp.where(at == target, 1.0, 0.0).astype(BF16)
    placed = jnp.dot(place, lanes[...], preferred_element_type=F32)
    for fetch in fetches[len(small) :]:
        fetch.wait()
    remain_ref[0] = image[...] - (placed[:, :256] + placed[:, 256:])

    def fold(value):
        total = value[0:8]
        for r in range(8, STAMP, 8):
            total = total + value[r : r + 8]
        return total

    sub = lax.broadcasted_iota(jnp.int32, (STAMP // 8 + 1, 8, 128), 1)
    none = jnp.zeros((1, 8, 128), F32)
    for j in range(pairs):
        at_x = row + pair_of(j, offset_ref, 0, 0, 0)
        at_y = column1 + pair_of(j, offset_ref, 1, 0, 0)
        inside = (at_x >= 0) & (at_x < tile) & (at_y >= 0) & (at_y < tile)
        own = slice(128 * j, 128 * (j + 1))
        masked = [jnp.where(inside, blurred[k, :, own], 0.0) for k in range(3)]
        steps = [jnp.bitwise_and(offset_ref[0, 0, 0, 2 * j + odd], 7) for odd in range(2)]
        for k in range(3):
            value = masked[k].reshape(STAMP // 8, 8, 128)
            moved = []
            for step in steps:
                turned = pltpu.roll(value, step, 1)
                moved.append(
                    jnp.where(
                        sub < step,
                        jnp.concatenate([none, turned], axis=0),
                        jnp.concatenate([turned, none], axis=0),
                    )
                )
            shifted[k, 9 * j : 9 * (j + 1)] = jnp.where(first_half, moved[0], moved[1])
        n = 0
        for k in range(3):
            for l in range(k, 3):
                partial[8 * n : 8 * (n + 1), own] = fold(masked[k] * masked[l])
                n += 1

    segment = jnp.where(
        jnp.right_shift(lax.broadcasted_iota(jnp.int32, (slots * STAMP, 128), 0), 6)
        == lax.broadcasted_iota(jnp.int32, (slots * STAMP, 128), 1),
        1.0,
        0.0,
    ).astype(BF16)

    def gather_sums(value):
        size = value.shape[0]
        out = jnp.dot(
            jnp.concatenate(split(value), axis=0), segment, preferred_element_type=F32
        )
        out = out[:size] + out[size:]
        return [
            jnp.sum(out[8 * k : 8 * (k + 1)], axis=0, keepdims=True) for k in range(size // 8)
        ]

    def shares_of(ref, send, recv):
        def share(slot, d):
            return pltpu.make_async_remote_copy(
                src_ref=ref.at[slot],
                dst_ref=ref.at[slot],
                send_sem=send.at[d - 1],
                recv_sem=recv.at[d - 1],
                device_id=peers[d - 1],
                device_id_type=MESH,
            )

        order = sorted(range(1, nb), key=lambda d: -min(d, nb - d))
        sent = [share(me, d) for d in order]
        for copy in sent:
            copy.start()
        return sent, [(share, lax.rem(me + nb - d, nb), d) for d in order]

    weight = weight_ref[0]
    normal = gather_sums(partial[0:48, :])
    normals[me] = weight * jnp.concatenate(normal + [jnp.zeros((2, 128), F32)], axis=0)
    sent, expected = shares_of(normals, normal_send, normal_recv)

    for r in range(MARGIN // 8):
        for g in range(2):
            blocks[r, g] = jnp.zeros((8, 128), F32)
            blocks[tile // 8 + MARGIN // 8 + r, g] = jnp.zeros((8, 128), F32)

    for d in range(8):

        @pl.when(exists[opposite[d]] == 1)
        def _():
            halos[d].wait_recv()

    ones = jnp.ones((1, 128), jnp.int32)
    has_up, has_down, has_left, has_right = [
        ones * there > 0 for there in (above, below, before, after)
    ]
    low_lanes = lane1 < MARGIN
    high_lanes = lane1 >= 128 - MARGIN

    def unpack(block, c, first_lane):
        turn = (first_lane + 128 - 32 * c) % 128
        return pltpu.roll(block, turn, 1) if turn else block

    def unpack_corner(block, first_lane):
        return jnp.concatenate([unpack(block, c, first_lane) for c in range(4)], axis=0)

    for c in range(4):
        for g in range(2):
            r0 = 64 * c
            own = slice(128 * g, 128 * (g + 1))
            if g == 0:
                total = jnp.where(low_lanes & has_left, unpack(in_sides[1], c, 0), 0.0)
            else:
                total = jnp.where(high_lanes & has_right, unpack(in_sides[0], c, 96), 0.0)
            if c == 0 or c == 3:
                there = has_up if c == 0 else has_down
                fringe = jnp.where(there, in_rows[1 if c == 0 else 0, :, own], 0.0)
                n = (3 if c == 0 else 1) - g
                corner = unpack_corner(in_corners[n], 96 * g)
                there = there & ((low_lanes & has_left) if g == 0 else (high_lanes & has_right))
                fringe = fringe + jnp.where(there, corner, 0.0)
                if c == 0:
                    total = jnp.concatenate([total[0:32] + fringe, total[32:64]], axis=0)
                else:
                    total = jnp.concatenate([total[0:32], total[32:64] + fringe], axis=0)
            value = remain_ref[0, r0 : r0 + 64, own] - total
            remain_ref[0, r0 : r0 + 64, own] = value
            for r in range(8):
                blocks[MARGIN // 8 + 8 * c + r, g] = value[8 * r : 8 * (r + 1)]

    for j in range(pairs):
        halves = []
        for odd in range(2):
            s = 2 * j + odd
            at_x = jnp.clip(offset_ref[0, 0, 0, s] + MARGIN, 0, tile - 1)
            first = jnp.right_shift(at_x, 3)
            at_y = offset_ref[1, 0, 0, s]
            turn = jnp.bitwise_and(at_y, 127)
            block = jnp.right_shift(at_y - turn, 7)
            take_one = jnp.where(lane1 >= turn, block, block + 1) >= 1
            value = jnp.stack(
                [
                    jnp.where(take_one, blocks[first + r, 1], blocks[first + r, 0])
                    for r in range(STAMP // 8 + 1)
                ]
            )
            value = pltpu.roll(value, jnp.bitwise_and(STAMP * odd + 256 - turn, 127), 2)
            halves.append(value)
        cutout = jnp.where(first_half, halves[0], halves[1])
        own = slice(128 * j, 128 * (j + 1))
        for k in range(3):
            partial[48 + 8 * k : 56 + 8 * k, own] = jnp.sum(
                shifted[k, 9 * j : 9 * (j + 1)] * cutout, axis=0
            )
    right = gather_sums(partial[48:72, :])
    right = right[0] + pltpu.roll(right[1], slots, 1) + pltpu.roll(right[2], 2 * slots, 1)
    rights[me] = weight * right
    more, others = shares_of(rights, right_send, right_recv)

    for halo, there in zip(halos, exists):

        @pl.when(there == 1)
        def _():
            halo.wait_send()

    for share in sent:
        share.wait_send()
    for share, slot, d in expected:
        share(slot, d).wait_recv()
    total = normals[0]
    for e in range(1, nb):
        total = total + normals[e]
    entry = [total[n : n + 1, 0:slots] for n in range(6)]
    live = lax.broadcasted_iota(jnp.int32, (1, slots), 1) < live_count
    flux = jnp.where(live, flux_vec[0], 0.0)
    m00, m01, m02 = entry[0] + PRIOR, entry[1] * flux, entry[2] * flux
    m11, m12 = entry[3] * flux * flux + PRIOR, entry[4] * flux * flux
    m22 = entry[5] * flux * flux + PRIOR
    c00 = m11 * m22 - m12 * m12
    c01 = m12 * m02 - m01 * m22
    c02 = m01 * m12 - m11 * m02
    c11 = m00 * m22 - m02 * m02
    c12 = m01 * m02 - m00 * m12
    c22 = m00 * m11 - m01 * m01
    scale = jnp.where(live, 1.0, 0.0) / (m00 * c00 + m01 * c01 + m02 * c02)
    rows = [c00, c01, c02, c01, c11, c12, c02, c12, c22]
    for n in range(9):
        sums_ref[n : n + 1, 0:slots] = rows[n] * (scale if n % 3 == 0 else scale * flux)
    bases = [flux_vec[0], shift_vec[0, 0], shift_vec[1, 0]]
    for k in range(3):
        sums_ref[9 + k : 10 + k, 0:slots] = jnp.where(live, bases[k], 0.0)

    for share, slot, d in others:
        share(slot, d).wait_recv()
    total = rights[0]
    for e in range(1, nb):
        total = total + rights[e]
    sums_ref[12:13] = total
    for share in more:
        share.wait_send()


def finish(sums_ref, remain_ref, refined_hbm, residual_hbm, refined, sems):
    store = pltpu.make_async_copy(remain_ref, residual_hbm, sems.at[0])
    store.start()
    slots = refined.shape[3]
    right = [sums_ref[12:13, slots * k : slots * (k + 1)] for k in range(3)]
    for k in range(3):
        value = sums_ref[9 + k : 10 + k, 0:slots]
        for l in range(3):
            value = value + sums_ref[3 * k + l : 3 * k + l + 1, 0:slots] * right[l]
        refined[k, 0] = value
    write = pltpu.make_async_copy(refined, refined_hbm, sems.at[1])
    write.start()
    store.wait()
    write.wait()


def shards(
    image,
    psf_taps,
    exposure_weight,
    flux_start,
    centre_shift,
    radius,
    ellipticity,
    offsets,
    source_count,
):
    tile = image.shape[1]
    slots = flux_start.shape[2]
    rows = tile + 2 * MARGIN
    width = slots * STAMP
    vmem = pl.BlockSpec(memory_space=pltpu.VMEM)
    hbm = pl.BlockSpec(memory_space=pl.ANY)
    peers = lax.axis_size("be") - 1
    smem = pl.BlockSpec(memory_space=pltpu.SMEM)
    fetched = (psf_taps, flux_start, centre_shift, radius, ellipticity, offsets)
    sums, remain = pl.pallas_call(
        kernel,
        out_shape=(pltpu.VMEM((16, 128), F32), pltpu.VMEM(image.shape, F32)),
        in_specs=[hbm] * 2 + [smem] + [hbm] * 5 + [smem],
        out_specs=(vmem, vmem),
        scratch_shapes=[pltpu.SMEM(operand.shape, operand.dtype) for operand in fetched]
        + [
            pltpu.VMEM(flux_start.shape, F32),
            pltpu.VMEM(centre_shift.shape, F32),
            pltpu.VMEM((tile, tile), F32),
            pltpu.VMEM((EDGES * STAMP, 768), BF16),
            pltpu.VMEM((2, MARGIN, tile), F32),
            pltpu.VMEM((2, STAMP, 128), F32),
            pltpu.VMEM((4, 8, 128), F32),
            pltpu.VMEM((2, MARGIN, tile), F32),
            pltpu.VMEM((2, STAMP, 128), F32),
            pltpu.VMEM((4, 8, 128), F32),
            pltpu.VMEM((3 * STAMP, 3 * width), BF16),
            pltpu.VMEM((3, STAMP, width), F32),
            pltpu.VMEM((width, 2 * tile), BF16),
            pltpu.VMEM((rows // 8, 2, 8, 128), F32),
            pltpu.VMEM((3, 9 * (slots // 2), 8, 128), F32),
            pltpu.VMEM((72, width), F32),
            pltpu.VMEM((peers + 1, 8, 128), F32),
            pltpu.VMEM((peers + 1, 1, 128), F32),
            pltpu.SemaphoreType.DMA((9,)),
            pltpu.SemaphoreType.DMA((8,)),
            pltpu.SemaphoreType.DMA((8,)),
            pltpu.SemaphoreType.DMA((peers,)),
            pltpu.SemaphoreType.DMA((peers,)),
            pltpu.SemaphoreType.DMA((peers,)),
            pltpu.SemaphoreType.DMA((peers,)),
        ],
        compiler_params=pltpu.CompilerParams(collective_id=0, has_side_effects=True),
        name="photometry",
    )(
        image,
        psf_taps,
        exposure_weight,
        flux_start,
        centre_shift,
        radius,
        ellipticity,
        offsets,
        source_count,
    )
    sums = pltpu.with_memory_space_constraint(sums, pltpu.VMEM)
    remain = pltpu.with_memory_space_constraint(remain, pltpu.VMEM)
    return pl.pallas_call(
        finish,
        out_shape=(
            jax.ShapeDtypeStruct((3, 1, 1, slots), F32),
            jax.ShapeDtypeStruct(image.shape, F32),
        ),
        in_specs=[vmem, vmem],
        out_specs=(hbm, hbm),
        scratch_shapes=[pltpu.VMEM((3, 1, 1, slots), F32), pltpu.SemaphoreType.DMA((2,))],
        name="finish",
    )(sums, remain)


def solution(mesh):
    return jax.shard_map(
        shards,
        mesh=mesh,
        in_specs=(
            P("be", "skyx", "skyy"),
            P("be", None, None),
            P("be"),
            P("skyx", "skyy", None),
            P(None, "skyx", "skyy", None),
            P("skyx", "skyy", None),
            P(None, "skyx", "skyy", None),
            P(None, "skyx", "skyy", None),
            P("skyx", "skyy"),
        ),
        out_specs=(P(None, "skyx", "skyy", None), P("be", "skyx", "skyy")),
        check_vma=False,
    )
```
